512 devices in a mesh: pairs: 64 (over x, z), grp: 8 (over y, core).
Axes of the slice: x: 4, y: 4, z: 16, core: 2. Of those that a mesh axis runs over, the one named last changes fastest.
Arguments:
- spectra: bfloat16 [8192, 1, 2048], P(('pairs', 'grp')), as said below
- row_station: int32 [8192], P(('pairs', 'grp')), may hold values from 0 to 4095, as said below
- row_window: int32 [8192], P(('pairs', 'grp')), may hold values from 0 to 1, as said below
- station_owner: int32 [4096], replicated, may hold values from 0 to 511, as said below
- tile_stations: int32 [64, 384], replicated, may hold values from 0 to 4095, as said below
- pair_index: int32 [64, 8, 2, 48], P('pairs', 'grp'), may hold values from 0 to 383
Outputs:
- correlation: float32 [64, 8, 48, 2001], P('pairs', 'grp')
The draws below stay inside these ranges and needn't reach their ends.
Inputs may be any that keep to these rules, and one draw needn't show every extreme that they name: `row_station`: every station's 2 windows lie on the device that station_owner names, one row each; every device holds 8 stations. `row_window`: A device's rows of one station carry each window number once. `station_owner`: devices are numbered by pairs index times the size of grp plus grp index. `tile_stations`: A group's list holds distinct stations on distinct devices; exactly 48 of them lie on devices of each grp index. `spectra`: real parts of the 1024 bins, then their imaginary parts.
All inputs are finite; a program needn't handle non-finite values.
Results may differ from the reference program's by a relative error of at most 0.0056.
Values may be sent and summed in bfloat16 or wider, within the bound.
A program may use at most 64 MiB of HBM per device.

```python
import math
import jax
import jax.numpy as jnp
from jax import lax

STA_DEV = 8
W = 2
NSEG = 1
NFFT = 2048
BAND = 128
MAXLAG = 1000
PPD = 48
PANEL = 48
STATIONS = 4096
USTA = 384
LAGS = 2001
N_PAIRS = 64
N_GRP = 8
DEVICES = 512


def distinct_order(key, full_shape):
    item_count = full_shape[-1]
    scores = jax.random.randint(key, full_shape, 0, 1 << 12) * item_count + jnp.arange(item_count, dtype=jnp.int32)
    return jnp.argsort(scores, axis=-1).astype(jnp.int32)


def station_layout(key):
    key_list = jax.random.split(jax.random.fold_in(key, 4711), 5)
    station_order = jax.random.permutation(key_list[0], STATIONS).astype(jnp.int32)
    by_device = station_order.reshape(DEVICES, STA_DEV)
    owner_map = jnp.zeros((STATIONS,), jnp.int32).at[station_order].set(jnp.arange(STATIONS, dtype=jnp.int32) // STA_DEV)
    local_count = STA_DEV * W
    item_order = distinct_order(key_list[1], (DEVICES, local_count))
    row_station = jnp.take_along_axis(by_device, item_order // W, axis=1).reshape(-1)
    row_window = (item_order % W).reshape(-1)
    picked = distinct_order(key_list[2], (N_PAIRS, N_GRP, N_PAIRS))[:, :, :PANEL]
    device_ids = picked * N_GRP + jnp.arange(N_GRP, dtype=jnp.int32)[None, :, None]
    which_station = jax.random.randint(key_list[3], (N_PAIRS, N_GRP, PANEL), 0, STA_DEV)
    listed = by_device[device_ids, which_station].reshape(N_PAIRS, USTA)
    shuffle_order = distinct_order(key_list[4], (N_PAIRS, USTA))
    tile_list = jnp.take_along_axis(listed, shuffle_order, axis=1)
    return (row_station, row_window, owner_map, tile_list)


def draw_row_station(key, part):
    return station_layout(key)[0]


def draw_row_window(key, part):
    return station_layout(key)[1]


def draw_station_owner(key, part):
    return station_layout(key)[2]


def draw_tile_stations(key, part):
    return station_layout(key)[3]


def draw_spectra(key, part):
    key_list = jax.random.split(jax.random.fold_in(key, 9157), 2)
    row_total = STA_DEV * DEVICES * W
    band_count = NFFT // 2 // BAND
    full_shape = (row_total, NSEG, 2, band_count, BAND)
    level_shape = (row_total, NSEG, 1, band_count, 1)
    values = jax.random.normal(key_list[0], full_shape, jnp.float32)
    band_level = jnp.exp(jax.random.uniform(key_list[1], level_shape, jnp.float32, 0.0, math.log(10.0)))
    return (values * band_level).reshape(row_total, NSEG, NFFT).astype(jnp.bfloat16)


def set_ends(result, key, smallest, high):
    extent = result.shape
    spot = [jax.random.randint(jax.random.fold_in(key, axis), (), 0, extent[axis]) for axis in range(len(extent))]
    result = result.at[tuple(spot)].set(smallest)
    longest = extent.index(max(extent))
    spot[longest] = (spot[longest] + 1) % extent[longest]
    return result.at[tuple(spot)].set(high)


def setup_inputs(seed: int = 0) -> dict:
    arg_keys = jax.random.split(jax.random.key(seed), 7)
    return {
        "spectra": draw_spectra(jax.random.fold_in(arg_keys[6], 71), 0),
        "row_station": draw_row_station(jax.random.fold_in(arg_keys[6], 71), 0),
        "row_window": draw_row_window(jax.random.fold_in(arg_keys[6], 71), 0),
        "station_owner": draw_station_owner(jax.random.fold_in(arg_keys[6], 71), 0),
        "tile_stations": draw_tile_stations(jax.random.fold_in(arg_keys[6], 71), 0),
        "pair_index": set_ends(jax.random.randint(arg_keys[5], (N_PAIRS, N_GRP, 2, PPD), 0, USTA), jax.random.fold_in(arg_keys[5], 1), 0, USTA - 1).astype(jnp.int32),
    }


freq_block_max = 512
power_eps = 1e-06

def whiten_rows(spectra, band_width):
    half_bins = spectra.shape[-1] // 2
    leading = spectra.shape[:-1]
    values = spectra.astype(jnp.float32).reshape(leading + (2, half_bins // band_width, band_width))
    band_power = lax.optimization_barrier(jnp.mean(lax.optimization_barrier(jnp.sum(values * values, axis=-3)), axis=-1))
    scaling = lax.rsqrt(band_power + power_eps)
    whitened = values * scaling[..., None, :, None]
    return whitened.reshape(spectra.shape).astype(jnp.bfloat16)

def lag_table(offset, bin_count):
    freq_index = (offset + jnp.arange(bin_count, dtype=jnp.int32))[:, None]
    lag_shift = (jnp.arange(LAGS, dtype=jnp.int32) + (NFFT - MAXLAG))[None, :]
    angles = (freq_index * lag_shift % NFFT).astype(jnp.float32) * (2.0 * math.pi / NFFT)
    return jnp.concatenate([jnp.cos(angles), -jnp.sin(angles)], axis=0).astype(jnp.bfloat16)

def cross_block(source_rows, first_rows, second_rows, offset, bin_count):
    half_bins = source_rows.shape[-1] // 2
    real_part = source_rows[:, :, offset:offset + bin_count]
    imag_part = source_rows[:, :, half_bins + offset:half_bins + offset + bin_count]
    real_a = real_part[first_rows].astype(jnp.float32)
    imag_a = imag_part[first_rows].astype(jnp.float32)
    real_b = real_part[second_rows].astype(jnp.float32)
    imag_b = imag_part[second_rows].astype(jnp.float32)
    cross_real = lax.optimization_barrier(jnp.sum(real_a * real_b + imag_a * imag_b, axis=(1, 2)))
    cross_imag = lax.optimization_barrier(jnp.sum(imag_a * real_b - real_a * imag_b, axis=(1, 2)))
    return jnp.concatenate([cross_real, cross_imag], axis=1).astype(jnp.bfloat16)

def correlate(source_rows, first_rows, second_rows, tables):
    half_bins = NFFT // 2
    block_size = min(freq_block_max, half_bins)
    running = jnp.zeros((first_rows.shape[0], LAGS), jnp.float32)
    for block_number, offset in enumerate(range(0, half_bins, block_size)):
        cross_terms = lax.optimization_barrier(cross_block(source_rows, first_rows, second_rows, offset, block_size))
        running = running + jnp.dot(cross_terms.astype(jnp.float32), tables[block_number], precision=lax.Precision.HIGHEST, preferred_element_type=jnp.float32)
    return running * (1.0 / math.sqrt(half_bins * W * NSEG))

def reference(spectra, row_station, row_window, station_owner, tile_stations, pair_index):
    whitened = whiten_rows(spectra, BAND)
    local_count = STA_DEV * W
    device_stations = row_station.reshape(DEVICES, local_count)
    device_windows = row_window.reshape(DEVICES, local_count)
    window_ids = jnp.arange(W, dtype=jnp.int32)
    local_ids = jnp.arange(local_count, dtype=jnp.int32)
    half_bins = NFFT // 2
    block_size = min(freq_block_max, half_bins)
    tables = [lax.optimization_barrier(lag_table(offset, block_size)).astype(jnp.float32) for offset in range(0, half_bins, block_size)]

    def one_group(group_args):
        stations, pair_lists = group_args
        owners = station_owner[stations]
        held_stations = device_stations[owners]
        held_windows = device_windows[owners]
        matched = (held_stations[:, None, :] == stations[:, None, None]) & (held_windows[:, None, :] == window_ids[None, :, None])
        local_slot = lax.optimization_barrier(jnp.sum(jnp.where(matched, local_ids, 0), axis=2)).astype(jnp.int32)
        located = owners[:, None] * local_count + local_slot
        first_rows = located[pair_lists[:, 0, :].reshape(-1)]
        second_rows = located[pair_lists[:, 1, :].reshape(-1)]
        return correlate(whitened, first_rows, second_rows, tables).reshape(N_GRP, PPD, LAGS)
    return lax.map(one_group, (tile_stations, pair_index))
```

```python
import math

import jax
import jax.numpy as jnp
from jax import lax
from jax.sharding import PartitionSpec as P

W = 2
NFFT = 2048
HALF = 1024
BAND = 128
BANDS = 8
MAXLAG = 1000
LAGS = 2001
power_eps = 1e-06


def whiten_rows(spectra):
    rows = spectra.shape[0]
    values = spectra.astype(jnp.float32).reshape(rows, 2, BANDS, BAND)
    band_power = jnp.mean(jnp.sum(values * values, axis=1), axis=-1)
    scaling = lax.rsqrt(band_power + power_eps)
    return (values * scaling[:, None, :, None]).astype(jnp.bfloat16)


def lag_table():
    freq = jnp.arange(HALF, dtype=jnp.int32)[:, None]
    step = 2.0 * math.pi / NFFT
    coarse = (jnp.arange(16, dtype=jnp.int32) * 128 + (NFFT - MAXLAG))[None, :]
    fine = jnp.arange(128, dtype=jnp.int32)[None, :]
    a = (freq * coarse % NFFT).astype(jnp.float32) * step
    b = (freq * fine % NFFT).astype(jnp.float32) * step
    ca, sa, cb, sb = lax.optimization_barrier((jnp.cos(a), jnp.sin(a), jnp.cos(b), jnp.sin(b)))
    ca, sa, cb, sb = ca[:, :, None], sa[:, :, None], cb[:, None, :], sb[:, None, :]
    real = (ca * cb - sa * sb).reshape(HALF, 2048)
    imag = -(sa * cb + ca * sb).reshape(HALF, 2048)
    table = jnp.stack([real.reshape(BANDS, BAND, 2048), imag.reshape(BANDS, BAND, 2048)], axis=1)
    return table.reshape(2 * HALF, 2048).astype(jnp.bfloat16)


def on_device(spectra, row_station, row_window, station_owner, tile_stations, pair_index):
    groups = lax.axis_size("pairs")
    members = lax.axis_size("grp")
    my_pair = lax.axis_index("pairs")
    local = spectra.shape[0]
    white = whiten_rows(spectra).reshape(local, 2 * HALF)
    wanted = jnp.any(row_station[None, :, None] == tile_stations[:, None, :], axis=2)
    window_hit = row_window[None, :] == jnp.arange(W, dtype=jnp.int32)[:, None]
    chosen = (wanted[:, None, :] & window_hit[None]).reshape(groups * W, local).astype(jnp.bfloat16)
    outgoing = jnp.dot(chosen, white, preferred_element_type=jnp.float32).astype(jnp.bfloat16)
    outgoing = outgoing.reshape(groups, W, 2, members, BAND).transpose(0, 3, 1, 2, 4)
    outgoing = outgoing.reshape(groups * members, W * 2 * BAND)
    arrived = lax.all_to_all(outgoing, ("pairs", "grp"), split_axis=0, concat_axis=0, tiled=True)
    pairs = pair_index.reshape(1, 2, -1)
    per_device = pairs.shape[2]
    pairs = lax.all_to_all(
        jnp.broadcast_to(pairs, (members,) + pairs.shape[1:]), "grp", split_axis=0, concat_axis=0, tiled=True
    )
    my_tile = lax.dynamic_index_in_dim(tile_stations, my_pair, 0, keepdims=False)
    owner = station_owner[my_tile]
    first = arrived[owner[pairs[:, 0].reshape(-1)]].astype(jnp.float32).reshape(-1, W, 2, BAND)
    second = arrived[owner[pairs[:, 1].reshape(-1)]].astype(jnp.float32).reshape(-1, W, 2, BAND)
    real = jnp.sum(first[:, :, 0] * second[:, :, 0] + first[:, :, 1] * second[:, :, 1], axis=1)
    imag = jnp.sum(first[:, :, 1] * second[:, :, 0] - first[:, :, 0] * second[:, :, 1], axis=1)
    cross = jnp.concatenate([real, imag], axis=1).astype(jnp.bfloat16)
    cross = cross.reshape(members, per_device, 2 * BAND)
    cross = lax.all_to_all(cross, "grp", split_axis=0, concat_axis=0, tiled=True)
    cross = cross.transpose(1, 0, 2).reshape(per_device, members * 2 * BAND)
    running = jnp.dot(cross, lag_table(), preferred_element_type=jnp.float32)[:, :LAGS]
    running = running * (1.0 / math.sqrt(HALF * W))
    return running.reshape(1, 1, per_device, LAGS)


def solution(mesh):
    placed = (
        P(("pairs", "grp"), None, None),
        P(("pairs", "grp")),
        P(("pairs", "grp")),
        P(),
        P(),
        P("pairs", "grp", None, None),
    )
    return jax.shard_map(
        on_device,
        mesh=mesh,
        in_specs=placed,
        out_specs=P("pairs", "grp", None, None),
        check_vma=False,
    )
```

```python
import math

import jax
import jax.numpy as jnp
from jax import lax
from jax.experimental import pallas as pl
from jax.experimental.pallas import tpu as pltpu
from jax.sharding import PartitionSpec as P

MESH = pl.DeviceIdType.MESH
W = 2
NFFT = 2048
HALF = 1024
MAXLAG = 1000
LAGS = 2001
EPS = 1e-06
NX = 4
NZ = 16
NG = 8
LAYER = NX * NG
STA = 8
PPD = 48
TOTAL = NZ * LAYER * STA
STEP = 2.0 * math.pi / NFFT
F32 = jnp.float32
I32 = jnp.int32
BF16 = jnp.bfloat16


def iota(shape, axis):
    return lax.broadcasted_iota(I32, shape, axis)


def angle(steps):
    return lax.rem(steps, NFFT).astype(F32) * STEP


def diagonal_column(row, size):
    same = iota((size, size), 0) == iota((size, size), 1)
    return jnp.sum(jnp.where(same, jnp.broadcast_to(row, (size, size)), 0), axis=1, keepdims=True)


def pack_rows(spec_ref, station_ref, window_ref, send_ref):
    station = station_ref[...]
    column = diagonal_column(station, 2 * STA)
    ahead = jnp.sum(jnp.where(column < station, 1, 0), axis=0, keepdims=True)
    place = window_ref[...] * STA + lax.div(ahead, W)
    order = jnp.where(iota((2 * STA, 2 * STA), 0) == place, 1.0, 0.0).astype(BF16)
    group = lax.div(iota((STA, 128), 1), 32)
    for tile in range(8):
        real = spec_ref[:, 128 * tile : 128 * tile + 128].astype(F32)
        imag = spec_ref[:, HALF + 128 * tile : HALF + 128 * tile + 128].astype(F32)
        power = jnp.sum(real * real + imag * imag, axis=1, keepdims=True) * (1.0 / 128)
        scale = lax.rsqrt(power + EPS)
        real = jnp.dot(order, (real * scale).astype(BF16), preferred_element_type=F32)
        imag = jnp.dot(order, (imag * scale).astype(BF16), preferred_element_type=F32)
        parts = (real[:STA], imag[:STA], real[STA:], imag[STA:])
        for quarter in range(4):
            piece = None
            for k in range(4):
                shift = (32 * (k - quarter)) % 128
                moved = pltpu.roll(parts[k], shift, 1) if shift else parts[k]
                piece = moved if piece is None else jnp.where(group == k, moved, piece)
            send_ref[4 * tile + quarter] = piece.astype(BF16)


def locate(pair_ref, tiles_ref, owner_ref, group):
    ends = 2 * PPD
    pairs = pair_ref[...]
    place = jnp.concatenate([diagonal_column(pairs[h : h + 1], PPD) for h in range(2)], axis=0)
    lanes = iota((ends, 128), 1)
    stations = tiles_ref[pl.ds(group, 1), :]
    found = jnp.zeros((ends, 128), I32)
    for c in range(3):
        found += jnp.where(place == lanes + 128 * c, stations[:, 128 * c : 128 * c + 128], 0)
    station = jnp.sum(found, axis=1, keepdims=True)
    found = jnp.zeros((ends, 128), I32)
    for c in range(32):
        found += jnp.where(station == lanes + 128 * c, owner_ref[c : c + 1, :], 0)
    owner = jnp.sum(found, axis=1, keepdims=True)
    found = jnp.zeros((ends, 128), I32)
    for c in range(32):
        ahead = (owner_ref[c : c + 1, :] == owner) & (lanes + 128 * c < station)
        found += jnp.where(ahead, 1, 0)
    rank = jnp.sum(found, axis=1, keepdims=True)
    part, member = lax.div(owner, NG), lax.rem(owner, NG)
    row = (lax.rem(part, NZ) * LAYER + lax.div(part, NZ) * NG + member) * STA + rank
    spread = jnp.where(iota((ends, 128), 0) == lanes, jnp.broadcast_to(row, (ends, 128)), 0)
    return jnp.sum(spread, axis=0, keepdims=True)


def build_table(table_ref, c8_ref, s8_ref, dc_ref, ds_ref):
    shift = NFFT - MAXLAG
    sub, lane = iota((8, 128), 0), iota((8, 128), 1)
    fine = angle(sub * (lane + shift))
    c0, s0 = jnp.cos(fine), jnp.sin(fine)
    coarse = angle(8 * iota((128, 128), 0) * (iota((128, 128), 1) + shift))
    c8_ref[...] = jnp.cos(coarse)
    s8_ref[...] = jnp.sin(coarse)
    for j in range(16):
        turn = angle(128 * j * sub)
        dc_ref[j] = jnp.cos(turn)
        ds_ref[j] = jnp.sin(turn)

    def block(u, carry):
        for h in range(2):
            base = []
            for q in range(2):
                v = 4 * u + 2 * h + q
                cv, sv = c8_ref[pl.ds(v, 1), :], s8_ref[pl.ds(v, 1), :]
                c, s = cv * c0 - sv * s0, sv * c0 + cv * s0
                base.append((c, s, -c, -s))
            for j in range(16):
                dc, ds = dc_ref[j], ds_ref[j]
                reals, imags = [], []
                for q in range(2):
                    c, s, nc, ns = base[q]
                    if q == 1 and j % 2 == 1:
                        c, s, nc, ns = nc, ns, c, s
                    reals.append(c * dc - s * ds)
                    imags.append(ns * dc + nc * ds)
                top = pl.multiple_of(64 * u + 16 * h, 16)
                low = pl.multiple_of(64 * u + 32 + 16 * h, 16)
                cols = slice(128 * j, 128 * j + 128)
                table_ref[pl.ds(top, 16), cols] = jnp.concatenate(reals, axis=0).astype(BF16)
                table_ref[pl.ds(low, 16), cols] = jnp.concatenate(imags, axis=0).astype(BF16)
        return carry

    lax.fori_loop(0, LAYER, block, 0)


def kernel(
    spec_ref, station_ref, window_ref, owner_ref, tiles_ref, pair_ref, out_ref,
    send_ref, rows_ref, wide_ref, index_ref, place_ref, first_ref, second_ref, cross_ref, got_ref, left_ref,
    table_ref, c8_ref, s8_ref, dc_ref, ds_ref,
    piece_send, piece_recv, index_send, index_recv, cross_send, cross_recv, ring_send, ring_recv, local_sem,
):
    group, member = lax.axis_index("pairs"), lax.axis_index("grp")
    x, z = lax.div(group, NZ), lax.rem(group, NZ)
    me = x * NG + member

    def device(number, layer):
        return (lax.div(number, NG) * NZ + layer, lax.rem(number, NG))

    def peer(j):
        return lax.rem(me + j, LAYER)

    ahead, behind = lax.rem(z + 1, NZ), lax.rem(z + NZ - 1, NZ)
    barrier = pltpu.get_barrier_semaphore()

    def greet(j, carry):
        pl.semaphore_signal(barrier, inc=1, device_id=device(peer(j), z), device_id_type=MESH)
        return carry

    lax.fori_loop(1, LAYER, greet, 0)
    pl.semaphore_signal(barrier, inc=1, device_id=device(me, ahead), device_id_type=MESH)
    pl.semaphore_signal(barrier, inc=1, device_id=device(me, behind), device_id_type=MESH)

    pack_rows(spec_ref, station_ref, window_ref, send_ref)
    index_ref[me] = locate(pair_ref, tiles_ref, owner_ref, group)
    rows_ref[z, me] = send_ref[me]
    pl.semaphore_wait(barrier, LAYER + 1)

    def piece_copy(number):
        return pltpu.make_async_remote_copy(
            src_ref=send_ref.at[number], dst_ref=rows_ref.at[z, me],
            send_sem=piece_send.at[number], recv_sem=piece_recv.at[me],
            device_id=device(number, z), device_id_type=MESH,
        )

    def piece_arrival(number):
        return pltpu.make_async_remote_copy(
            src_ref=send_ref.at[number], dst_ref=rows_ref.at[z, number],
            send_sem=piece_send.at[number], recv_sem=piece_recv.at[number],
            device_id=device(number, z), device_id_type=MESH,
        )

    def index_copy(number, source):
        return pltpu.make_async_remote_copy(
            src_ref=index_ref.at[me], dst_ref=index_ref.at[source],
            send_sem=index_send.at[number], recv_sem=index_recv.at[source],
            device_id=device(number, z), device_id_type=MESH,
        )

    def cross_copy(number, source):
        return pltpu.make_async_remote_copy(
            src_ref=cross_ref.at[number], dst_ref=got_ref.at[source],
            send_sem=cross_send.at[number], recv_sem=cross_recv.at[source],
            device_id=device(number, z), device_id_type=MESH,
        )

    def send_pieces(j, carry):
        piece_copy(peer(j)).start()
        return carry

    lax.fori_loop(1, LAYER, send_pieces, 0)

    def send_index(j, carry):
        index_copy(peer(j), me).start()
        return carry

    lax.fori_loop(1, LAYER, send_index, 0)

    build_table(table_ref, c8_ref, s8_ref, dc_ref, ds_ref)

    def ring_copy(way, d, s, chunk):
        part = pl.ds(NG * s, NG)
        return pltpu.make_async_remote_copy(
            src_ref=rows_ref.at[chunk, part], dst_ref=rows_ref.at[chunk, part],
            send_sem=ring_send.at[way, d, s], recv_sem=ring_recv.at[way, d, s],
            device_id=device(me, ahead if way == 0 else behind), device_id_type=MESH,
        )

    def widen(chunk, s):
        start = pl.multiple_of((chunk * LAYER + s * NG) * STA, 64)
        wide_ref[pl.ds(start, NG * STA), :] = rows_ref[chunk, pl.ds(NG * s, NG)].astype(F32).reshape(NG * STA, 128)

    def chunk_of(way, d):
        return lax.rem(z + NZ - d, NZ) if way == 0 else lax.rem(z + d, NZ)

    for k in range(NX):
        s = lax.rem(x + k, NX)

        def arrival(m, carry):
            number = s * NG + m

            @pl.when(number != me)
            def _():
                piece_arrival(number).wait_recv()

            return carry

        lax.fori_loop(0, NG, arrival, 0)
        ring_copy(0, 0, s, z).start()
        ring_copy(1, 0, s, z).start()
        widen(z, s)

    def index_arrival(j, carry):
        number = peer(j)
        index_copy(number, number).wait_recv()
        return carry

    lax.fori_loop(1, LAYER, index_arrival, 0)
    to_scalar = pltpu.make_async_copy(index_ref, place_ref, local_sem)
    to_scalar.start()

    def hop(d, carry):
        for k in range(NX):
            s = lax.rem(x + k, NX)
            for way in range(2):
                chunk = chunk_of(way, d + 1)
                ring_copy(way, d, s, chunk).wait_recv()
                ring_copy(way, d + 1, s, chunk).start()
                widen(chunk, s)
        return carry

    lax.fori_loop(0, 6, hop, 0)
    for k in range(NX):
        s = lax.rem(x + k, NX)
        for way in range(2):
            chunk = chunk_of(way, 7)
            ring_copy(way, 6, s, chunk).wait_recv()
            if (k < 2) == (way == 0):
                ring_copy(way, 7, s, chunk).start()
            widen(chunk, s)
    for k in range(NX):
        s = lax.rem(x + k, NX)
        way = 0 if k < 2 else 1
        chunk = chunk_of(way, 8)
        ring_copy(way, 7, s, chunk).wait_recv()
        widen(chunk, s)
    to_scalar.wait()

    lane = iota((PPD, 128), 1)
    odd = lax.rem(lax.div(lane, 32), 2) == 1
    low = iota((PPD // 2, 128), 1) < 64

    def correlate(j, carry):
        number = peer(j)
        for k in range(PPD):
            first = jnp.clip(place_ref[number, 0, k], 0, TOTAL - 1)
            second = jnp.clip(place_ref[number, 0, PPD + k], 0, TOTAL - 1)
            first_ref[k : k + 1, :] = wide_ref[pl.ds(first, 1), :]
            second_ref[k : k + 1, :] = wide_ref[pl.ds(second, 1), :]
        a, b = first_ref[...], second_ref[...]
        turned = jnp.where(odd, pltpu.roll(b, 32, 1), -pltpu.roll(b, 96, 1))
        real, imag = a * b, a * turned
        real = real + pltpu.roll(real, 64, 1)
        real = real + pltpu.roll(real, 32, 1)
        imag = imag + pltpu.roll(imag, 64, 1)
        imag = imag + pltpu.roll(imag, 32, 1)
        both = jnp.where(odd, imag, real)
        packed = jnp.where(low, both[: PPD // 2], both[PPD // 2 :])
        cross_ref[number] = packed.astype(BF16).reshape(3, 8, 128)

        @pl.when(j > 1)
        def _():
            cross_copy(peer(j - 1), me).start()

        return carry

    lax.fori_loop(1, LAYER + 1, correlate, 0)
    got_ref[me] = cross_ref[me]

    def cross_arrival(j, carry):
        number = peer(j)
        cross_copy(number, number).wait_recv()
        return carry

    lax.fori_loop(1, LAYER, cross_arrival, 0)

    for i in range(LAYER // 2):
        one = got_ref[2 * i].astype(F32).reshape(PPD // 2, 128)
        two = got_ref[2 * i + 1].astype(F32).reshape(PPD // 2, 128)
        top = jnp.where(low, one, pltpu.roll(two, 64, 1))
        bottom = jnp.where(low, pltpu.roll(one, 64, 1), two)
        left_ref[:, 128 * i : 128 * i + 128] = jnp.concatenate([top, bottom], axis=0).astype(BF16)

    scale = 1.0 / math.sqrt(HALF * W)

    def product(n, carry):
        cols = pl.ds(pl.multiple_of(256 * n, 256), 256)
        out_ref[:, cols] = jnp.dot(left_ref[...], table_ref[:, cols], preferred_element_type=F32) * scale
        return carry

    lax.fori_loop(0, 7, product, 0)
    tail = jnp.dot(left_ref[...], table_ref[:, 1792:2048], preferred_element_type=F32) * scale
    out_ref[:, 1792:LAGS] = tail[:, : LAGS - 1792]

    def sent(j, carry):
        number = peer(j)
        piece_copy(number).wait_send()
        index_copy(number, me).wait_send()
        cross_copy(number, me).wait_send()
        return carry

    lax.fori_loop(1, LAYER, sent, 0)

    def ring_sent(d, carry):
        for s in range(NX):
            for way in range(2):
                ring_copy(way, d, s, z).wait_send()
        return carry

    lax.fori_loop(0, 7, ring_sent, 0)
    for k in range(NX):
        s = lax.rem(x + k, NX)
        ring_copy(0 if k < 2 else 1, 7, s, z).wait_send()


def on_device(spectra, row_station, row_window, station_owner, tile_stations, pair_index):
    vmem = pl.BlockSpec(memory_space=pltpu.VMEM)
    dma = pltpu.SemaphoreType.DMA
    result = pl.pallas_call(
        kernel,
        out_shape=jax.ShapeDtypeStruct((PPD, LAGS), F32),
        in_specs=[vmem] * 6,
        out_specs=vmem,
        scratch_shapes=[
            pltpu.VMEM((LAYER, STA, 128), BF16),
            pltpu.VMEM((NZ, LAYER, STA, 128), BF16),
            pltpu.VMEM((TOTAL, 128), F32),
            pltpu.VMEM((LAYER, 1, 128), I32),
            pltpu.SMEM((LAYER, 1, 128), I32),
            pltpu.VMEM((PPD, 128), F32),
            pltpu.VMEM((PPD, 128), F32),
            pltpu.VMEM((LAYER, 3, 8, 128), BF16),
            pltpu.VMEM((LAYER, 3, 8, 128), BF16),
            pltpu.VMEM((PPD, NFFT), BF16),
            pltpu.VMEM((NFFT, NFFT), BF16),
            pltpu.VMEM((128, 128), F32),
            pltpu.VMEM((128, 128), F32),
            pltpu.VMEM((16, 8, 128), F32),
            pltpu.VMEM((16, 8, 128), F32),
            dma((LAYER,)),
            dma((LAYER,)),
            dma((LAYER,)),
            dma((LAYER,)),
            dma((LAYER,)),
            dma((LAYER,)),
            dma((2, 8, NX)),
            dma((2, 8, NX)),
            dma,
        ],
        compiler_params=pltpu.CompilerParams(
            collective_id=0, has_side_effects=True, vmem_limit_bytes=48 * 1024 * 1024
        ),
    )(
        spectra.reshape(2 * STA, NFFT),
        row_station.reshape(1, 2 * STA),
        row_window.reshape(1, 2 * STA),
        station_owner.reshape(32, 128),
        tile_stations,
        pair_index.reshape(2, PPD),
    )
    return result.reshape(1, 1, PPD, LAGS)


def solution(mesh):
    placed = (
        P(("pairs", "grp"), None, None),
        P(("pairs", "grp")),
        P(("pairs", "grp")),
        P(),
        P(),
        P("pairs", "grp", None, None),
    )
    return jax.shard_map(
        on_device,
        mesh=mesh,
        in_specs=placed,
        out_specs=P("pairs", "grp", None, None),
        check_vma=False,
    )
```

```python
import math

import jax
import jax.numpy as jnp
from jax import lax
from jax.experimental import pallas as pl
from jax.experimental.pallas import tpu as pltpu
from jax.sharding import PartitionSpec as P

MESH = pl.DeviceIdType.MESH
W = 2
NFFT = 2048
HALF = 1024
MAXLAG = 1000
LAGS = 2001
EPS = 1e-06
NX = 4
NZ = 16
NG = 8
LAYER = NX * NG
STA = 8
PPD = 48
TOTAL = NZ * LAYER * STA
HALVES = 2
PART = LAYER // HALVES
STEP = 2.0 * math.pi / NFFT
F32 = jnp.float32
I32 = jnp.int32
BF16 = jnp.bfloat16


def iota(shape, axis):
    return lax.broadcasted_iota(I32, shape, axis)


def angle(steps):
    return lax.rem(steps, NFFT).astype(F32) * STEP


def diagonal_column(row, size):
    same = iota((size, size), 0) == iota((size, size), 1)
    return jnp.sum(jnp.where(same, jnp.broadcast_to(row, (size, size)), 0), axis=1, keepdims=True)


def pack_rows(spec_ref, station_ref, window_ref, send_ref):
    station = station_ref[...]
    column = diagonal_column(station, 2 * STA)
    ahead = jnp.sum(jnp.where(column < station, 1, 0), axis=0, keepdims=True)
    place = window_ref[...] * STA + lax.div(ahead, W)
    order = jnp.where(iota((2 * STA, 2 * STA), 0) == place, 1.0, 0.0).astype(BF16)
    group = lax.div(iota((STA, 128), 1), 32)
    for tile in range(8):
        real = spec_ref[:, 128 * tile : 128 * tile + 128].astype(F32)
        imag = spec_ref[:, HALF + 128 * tile : HALF + 128 * tile + 128].astype(F32)
        power = jnp.sum(real * real + imag * imag, axis=1, keepdims=True) * (1.0 / 128)
        scale = lax.rsqrt(power + EPS)
        real = jnp.dot(order, (real * scale).astype(BF16), preferred_element_type=F32)
        imag = jnp.dot(order, (imag * scale).astype(BF16), preferred_element_type=F32)
        parts = (real[:STA], imag[:STA], real[STA:], imag[STA:])
        for quarter in range(4):
            piece = None
            for k in range(4):
                shift = (32 * (k - quarter)) % 128
                moved = pltpu.roll(parts[k], shift, 1) if shift else parts[k]
                piece = moved if piece is None else jnp.where(group == k, moved, piece)
            send_ref[4 * tile + quarter] = piece.astype(BF16)


def locate(pair_ref, tiles_ref, owner_ref, group):
    ends = 2 * PPD
    pairs = pair_ref[...]
    place = jnp.concatenate([diagonal_column(pairs[h : h + 1], PPD) for h in range(2)], axis=0)
    lanes = iota((ends, 128), 1)
    stations = tiles_ref[pl.ds(group, 1), :]
    found = jnp.zeros((ends, 128), I32)
    for c in range(3):
        found += jnp.where(place == lanes + 128 * c, stations[:, 128 * c : 128 * c + 128], 0)
    station = jnp.sum(found, axis=1, keepdims=True)
    found = jnp.zeros((ends, 128), I32)
    for c in range(32):
        found += jnp.where(station == lanes + 128 * c, owner_ref[c : c + 1, :], 0)
    owner = jnp.sum(found, axis=1, keepdims=True)
    found = jnp.zeros((ends, 128), I32)
    for c in range(32):
        ahead = (owner_ref[c : c + 1, :] == owner) & (lanes + 128 * c < station)
        found += jnp.where(ahead, 1, 0)
    rank = jnp.sum(found, axis=1, keepdims=True)
    part, member = lax.div(owner, NG), lax.rem(owner, NG)
    row = (lax.rem(part, NZ) * LAYER + lax.div(part, NZ) * NG + member) * STA + rank
    spread = jnp.where(iota((ends, 128), 0) == lanes, jnp.broadcast_to(row, (ends, 128)), 0)
    return jnp.sum(spread, axis=0, keepdims=True)


def table_angles(c8_ref, s8_ref, dc_ref, ds_ref, base_ref):
    shift = NFFT - MAXLAG
    sub, lane = iota((8, 128), 0), iota((8, 128), 1)
    fine = angle(sub * (lane + shift))
    base_ref[0] = jnp.cos(fine)
    base_ref[1] = jnp.sin(fine)
    coarse = angle(8 * iota((128, 128), 0) * (iota((128, 128), 1) + shift))
    c8_ref[...] = jnp.cos(coarse)
    s8_ref[...] = jnp.sin(coarse)
    for j in range(16):
        turn = angle(128 * j * sub)
        dc_ref[j] = jnp.cos(turn)
        ds_ref[j] = jnp.sin(turn)


def build_table(start, stop, table_ref, c8_ref, s8_ref, dc_ref, ds_ref, base_ref):
    def block(u, carry):
        c0, s0 = base_ref[0], base_ref[1]
        for h in range(2):
            base = []
            for q in range(2):
                v = 4 * u + 2 * h + q
                cv, sv = c8_ref[pl.ds(v, 1), :], s8_ref[pl.ds(v, 1), :]
                c, s = cv * c0 - sv * s0, sv * c0 + cv * s0
                base.append((c, s, -c, -s))
            for j in range(16):
                dc, ds = dc_ref[j], ds_ref[j]
                reals, imags = [], []
                for q in range(2):
                    c, s, nc, ns = base[q]
                    if q == 1 and j % 2 == 1:
                        c, s, nc, ns = nc, ns, c, s
                    reals.append(c * dc - s * ds)
                    imags.append(ns * dc + nc * ds)
                top = pl.multiple_of(64 * u + 16 * h, 16)
                low = pl.multiple_of(64 * u + 32 + 16 * h, 16)
                cols = slice(128 * j, 128 * j + 128)
                table_ref[pl.ds(top, 16), cols] = jnp.concatenate(reals, axis=0).astype(BF16)
                table_ref[pl.ds(low, 16), cols] = jnp.concatenate(imags, axis=0).astype(BF16)
        return carry

    lax.fori_loop(start, stop, block, 0)


def kernel(
    spec_hbm, station_hbm, window_hbm, owner_hbm, tiles_hbm, pair_hbm, out_ref,
    spec_ref, station_ref, window_ref, owner_ref, tiles_ref, pair_ref,
    send_ref, rows_ref, wide_ref, index_ref, place_ref, first_ref, second_ref, cross_ref, got_ref, left_ref,
    table_ref, c8_ref, s8_ref, dc_ref, ds_ref, base_ref,
    piece_send, piece_recv, index_send, index_recv, cross_send, cross_recv, ring_send, ring_recv, load_sem, local_sem,
):
    group, member = lax.axis_index("pairs"), lax.axis_index("grp")
    x, z = lax.div(group, NZ), lax.rem(group, NZ)
    me = x * NG + member
    sources = (spec_hbm, station_hbm, window_hbm, owner_hbm, tiles_hbm, pair_hbm)
    targets = (spec_ref, station_ref, window_ref, owner_ref, tiles_ref, pair_ref)
    loads = [pltpu.make_async_copy(a, b, load_sem.at[n]) for n, (a, b) in enumerate(zip(sources, targets))]
    for load in loads:
        load.start()

    def device(number, layer):
        return (lax.div(number, NG) * NZ + layer, lax.rem(number, NG))

    def peer(j):
        t = lax.div(j, NG)
        along = jnp.where(t == 0, 2, jnp.where(t == 1, 1, jnp.where(t == 2, 3, 0)))
        return lax.rem(x + along, NX) * NG + lax.rem(member + 2 * NG - 1 - lax.rem(j, NG), NG)

    def layer_at(offset):
        return lax.rem(z + NZ + offset, NZ)

    barrier = pltpu.get_barrier_semaphore()

    def greet(j, carry):
        pl.semaphore_signal(barrier, inc=1, device_id=device(peer(j), z), device_id_type=MESH)
        return carry

    for offset in (2, -2, 1, -1):
        pl.semaphore_signal(barrier, inc=1, device_id=device(me, layer_at(offset)), device_id_type=MESH)
    lax.fori_loop(0, LAYER - 1, greet, 0)

    for load in loads[:3]:
        load.wait()
    pack_rows(spec_ref, station_ref, window_ref, send_ref)
    rows_ref[z, me] = send_ref[me]
    for load in loads[3:]:
        load.wait()
    pl.semaphore_wait(barrier, LAYER - 1 + 4)

    def piece_copy(number):
        return pltpu.make_async_remote_copy(
            src_ref=send_ref.at[number], dst_ref=rows_ref.at[z, me],
            send_sem=piece_send.at[number], recv_sem=piece_recv.at[me],
            device_id=device(number, z), device_id_type=MESH,
        )

    def piece_arrival(number):
        return pltpu.make_async_remote_copy(
            src_ref=send_ref.at[number], dst_ref=rows_ref.at[z, number],
            send_sem=piece_send.at[number], recv_sem=piece_recv.at[number],
            device_id=device(number, z), device_id_type=MESH,
        )

    def index_copy(number, source):
        return pltpu.make_async_remote_copy(
            src_ref=index_ref.at[me], dst_ref=index_ref.at[source],
            send_sem=index_send.at[number], recv_sem=index_recv.at[source],
            device_id=device(number, z), device_id_type=MESH,
        )

    def cross_copy(number, source):
        return pltpu.make_async_remote_copy(
            src_ref=cross_ref.at[number], dst_ref=got_ref.at[source],
            send_sem=cross_send.at[number], recv_sem=cross_recv.at[source],
            device_id=device(number, z), device_id_type=MESH,
        )

    def send_pieces(j, carry):
        piece_copy(peer(j)).start()
        return carry

    lax.fori_loop(0, LAYER - 1, send_pieces, 0)
    index_ref[me] = locate(pair_ref, tiles_ref, owner_ref, group)
    table_angles(c8_ref, s8_ref, dc_ref, ds_ref, base_ref)

    def send_index(j, carry):
        index_copy(peer(j), me).start()
        return carry

    lax.fori_loop(0, LAYER - 1, send_index, 0)

    def table_part(start, stop):
        build_table(start, stop, table_ref, c8_ref, s8_ref, dc_ref, ds_ref, base_ref)

    def ring_copy(way, distance, s, chunk, step):
        part = pl.ds(PART * s, PART)
        return pltpu.make_async_remote_copy(
            src_ref=rows_ref.at[chunk, part], dst_ref=rows_ref.at[chunk, part],
            send_sem=ring_send.at[way, distance, s], recv_sem=ring_recv.at[way, distance, s],
            device_id=device(me, layer_at(step if way == 0 else -step)), device_id_type=MESH,
        )

    def widen(chunk, s):
        start = pl.multiple_of((chunk * LAYER + s * PART) * STA, 128)
        rows = rows_ref[chunk, pl.ds(PART * s, PART)].astype(F32)
        wide_ref[pl.ds(start, PART * STA), :] = rows.reshape(PART * STA, 128)

    def chunk_of(way, distance):
        return lax.rem(z + NZ - distance, NZ) if way == 0 else lax.rem(z + distance, NZ)

    def half(k):
        return lax.rem(lax.div(x, 2) + k, HALVES)

    def start_half(k, carry):
        s = half(k)

        def arrival(m, c):
            number = s * PART + m

            @pl.when(number != me)
            def _():
                piece_arrival(number).wait_recv()

            return c

        lax.fori_loop(0, PART, arrival, 0)
        for way in range(2):
            ring_copy(way, 2, s, z, 2).start()
            ring_copy(way, 1, s, z, 1).start()
        return carry

    lax.fori_loop(0, HALVES, start_half, 0)
    for s in range(HALVES):
        widen(z, s)
    table_part(0, 6)

    def index_arrival(j, carry):
        number = peer(j)
        index_copy(number, number).wait_recv()
        return carry

    lax.fori_loop(0, LAYER - 1, index_arrival, 0)
    to_scalar = pltpu.make_async_copy(index_ref, place_ref, local_sem)
    to_scalar.start()

    def stop(i, carry):
        distance = 2 * i + 2

        def one_half(k, c):
            s = half(k)
            for way in range(2):
                chunk = chunk_of(way, distance)

                @pl.when((distance < 8) | (k == way))
                def _():
                    ring_copy(way, distance, s, chunk, 2).wait_recv()

                @pl.when((distance < 6) | ((distance == 6) & (k == way)))
                def _():
                    ring_copy(way, distance + 2, s, chunk, 2).start()

                @pl.when(distance < 8)
                def _():
                    ring_copy(way, distance + 1, s, chunk, 1).start()

                @pl.when((distance < 8) | (k == way))
                def _():
                    widen(chunk, s)
            return c

        lax.fori_loop(0, HALVES, one_half, 0)

        def odd_half(k, c):
            s = half(k)
            for way in range(2):
                chunk = chunk_of(way, distance - 1)
                ring_copy(way, distance - 1, s, chunk, 1).wait_recv()
                widen(chunk, s)
            return c

        lax.fori_loop(0, HALVES, odd_half, 0)

        @pl.when(distance < 8)
        def _():
            table_part(6 + 9 * i, jnp.minimum(15 + 9 * i, LAYER))

        return carry

    lax.fori_loop(0, 4, stop, 0)
    to_scalar.wait()

    lane = iota((PPD, 128), 1)
    odd = lax.rem(lax.div(lane, 32), 2) == 1
    low = iota((PPD // 2, 128), 1) < 64

    def correlate(j, carry):
        number = peer(j)
        for k in range(PPD):
            first = place_ref[number, 0, k] & (TOTAL - 1)
            second = place_ref[number, 0, PPD + k] & (TOTAL - 1)
            first_ref[k : k + 1, :] = wide_ref[pl.ds(first, 1), :]
            second_ref[k : k + 1, :] = wide_ref[pl.ds(second, 1), :]
        a, b = first_ref[...], second_ref[...]
        turned = jnp.where(odd, pltpu.roll(b, 32, 1), -pltpu.roll(b, 96, 1))
        real, imag = a * b, a * turned
        real = real + pltpu.roll(real, 64, 1)
        real = real + pltpu.roll(real, 32, 1)
        imag = imag + pltpu.roll(imag, 64, 1)
        imag = imag + pltpu.roll(imag, 32, 1)
        both = jnp.where(odd, imag, real)
        packed = jnp.where(low, both[: PPD // 2], both[PPD // 2 :])
        cross_ref[number] = packed.astype(BF16).reshape(3, 8, 128)

        @pl.when(j > 0)
        def _():
            cross_copy(peer(j - 1), me).start()

        return carry

    lax.fori_loop(0, LAYER, correlate, 0)
    got_ref[me] = cross_ref[me]

    def cross_arrival(j, carry):
        number = peer(j)
        cross_copy(number, number).wait_recv()
        return carry

    lax.fori_loop(0, LAYER - 1, cross_arrival, 0)

    for i in range(LAYER // 2):
        one = got_ref[2 * i].astype(F32).reshape(PPD // 2, 128)
        two = got_ref[2 * i + 1].astype(F32).reshape(PPD // 2, 128)
        top = jnp.where(low, one, pltpu.roll(two, 64, 1))
        bottom = jnp.where(low, pltpu.roll(one, 64, 1), two)
        left_ref[:, 128 * i : 128 * i + 128] = jnp.concatenate([top, bottom], axis=0).astype(BF16)

    scale = 1.0 / math.sqrt(HALF * W)

    def product(n, carry):
        cols = pl.ds(pl.multiple_of(256 * n, 256), 256)
        out_ref[:, cols] = jnp.dot(left_ref[...], table_ref[:, cols], preferred_element_type=F32) * scale
        return carry

    lax.fori_loop(0, 7, product, 0)
    tail = jnp.dot(left_ref[...], table_ref[:, 1792:2048], preferred_element_type=F32) * scale
    out_ref[:, 1792:LAGS] = tail[:, : LAGS - 1792]

    def sent(j, carry):
        number = peer(j)
        piece_copy(number).wait_send()
        index_copy(number, me).wait_send()
        cross_copy(number, me).wait_send()
        return carry

    lax.fori_loop(0, LAYER - 1, sent, 0)

    def ring_sent(i, carry):
        distance, k = lax.div(i, HALVES) + 1, lax.rem(i, HALVES)
        for way in range(2):

            @pl.when((distance < 8) | (k == way))
            def _():
                ring_copy(way, distance, half(k), z, 1).wait_send()

        return carry

    lax.fori_loop(0, 8 * HALVES, ring_sent, 0)


def on_device(spectra, row_station, row_window, station_owner, tile_stations, pair_index):
    vmem = pl.BlockSpec(memory_space=pltpu.VMEM)
    dma = pltpu.SemaphoreType.DMA
    result = pl.pallas_call(
        kernel,
        out_shape=jax.ShapeDtypeStruct((PPD, LAGS), F32),
        in_specs=[pl.BlockSpec(memory_space=pl.ANY)] * 6,
        out_specs=vmem,
        scratch_shapes=[
            pltpu.VMEM((2 * STA, NFFT), BF16),
            pltpu.VMEM((1, 2 * STA), I32),
            pltpu.VMEM((1, 2 * STA), I32),
            pltpu.VMEM((32, 128), I32),
            pltpu.VMEM((NX * NZ, NG * PPD), I32),
            pltpu.VMEM((2, PPD), I32),
            pltpu.VMEM((LAYER, STA, 128), BF16),
            pltpu.VMEM((NZ, LAYER, STA, 128), BF16),
            pltpu.VMEM((TOTAL, 128), F32),
            pltpu.VMEM((LAYER, 1, 128), I32),
            pltpu.SMEM((LAYER, 1, 128), I32),
            pltpu.VMEM((PPD, 128), F32),
            pltpu.VMEM((PPD, 128), F32),
            pltpu.VMEM((LAYER, 3, 8, 128), BF16),
            pltpu.VMEM((LAYER, 3, 8, 128), BF16),
            pltpu.VMEM((PPD, NFFT), BF16),
            pltpu.VMEM((NFFT, NFFT), BF16),
            pltpu.VMEM((128, 128), F32),
            pltpu.VMEM((128, 128), F32),
            pltpu.VMEM((16, 8, 128), F32),
            pltpu.VMEM((16, 8, 128), F32),
            pltpu.VMEM((2, 8, 128), F32),
            dma((LAYER,)),
            dma((LAYER,)),
            dma((LAYER,)),
            dma((LAYER,)),
            dma((LAYER,)),
            dma((LAYER,)),
            dma((2, 9, HALVES)),
            dma((2, 9, HALVES)),
            dma((6,)),
            dma,
        ],
        compiler_params=pltpu.CompilerParams(
            collective_id=0, has_side_effects=True, vmem_limit_bytes=62 * 1024 * 1024
        ),
    )(
        spectra.reshape(2 * STA, NFFT),
        row_station.reshape(1, 2 * STA),
        row_window.reshape(1, 2 * STA),
        station_owner.reshape(32, 128),
        tile_stations,
        pair_index.reshape(2, PPD),
    )
    return result.reshape(1, 1, PPD, LAGS)


def solution(mesh):
    placed = (
        P(("pairs", "grp"), None, None),
        P(("pairs", "grp")),
        P(("pairs", "grp")),
        P(),
        P(),
        P("pairs", "grp", None, None),
    )
    return jax.shard_map(
        on_device,
        mesh=mesh,
        in_specs=placed,
        out_specs=P("pairs", "grp", None, None),
        check_vma=False,
    )
```

```python
import math

import jax
import jax.numpy as jnp
from jax import lax
from jax.experimental import pallas as pl
from jax.experimental.pallas import tpu as pltpu
from jax.sharding import PartitionSpec as P

MESH = pl.DeviceIdType.MESH
W = 2
NFFT = 2048
HALF = 1024
MAXLAG = 1000
LAGS = 2001
EPS = 1e-06
NX = 4
NZ = 16
NG = 8
LAYER = NX * NG
STA = 8
PPD = 48
TOTAL = NZ * LAYER * STA
HALVES = 2
PART = LAYER // HALVES
STEP = 2.0 * math.pi / NFFT
F32 = jnp.float32
I32 = jnp.int32
BF16 = jnp.bfloat16


def iota(shape, axis):
    return lax.broadcasted_iota(I32, shape, axis)


def angle(steps):
    return lax.rem(steps, NFFT).astype(F32) * STEP


def diagonal_column(row, size):
    same = iota((size, size), 0) == iota((size, size), 1)
    return jnp.sum(jnp.where(same, jnp.broadcast_to(row, (size, size)), 0), axis=1, keepdims=True)


def pack_rows(spec_ref, station_ref, window_ref, send_ref):
    station = station_ref[...]
    column = diagonal_column(station, 2 * STA)
    ahead = jnp.sum(jnp.where(column < station, 1, 0), axis=0, keepdims=True)
    place = window_ref[...] * STA + lax.div(ahead, W)
    order = jnp.where(iota((2 * STA, 2 * STA), 0) == place, 1.0, 0.0).astype(BF16)
    group = lax.div(iota((STA, 128), 1), 32)
    for tile in range(8):
        real = spec_ref[:, 128 * tile : 128 * tile + 128].astype(F32)
        imag = spec_ref[:, HALF + 128 * tile : HALF + 128 * tile + 128].astype(F32)
        power = jnp.sum(real * real + imag * imag, axis=1, keepdims=True) * (1.0 / 128)
        scale = lax.rsqrt(power + EPS)
        real = jnp.dot(order, (real * scale).astype(BF16), preferred_element_type=F32)
        imag = jnp.dot(order, (imag * scale).astype(BF16), preferred_element_type=F32)
        parts = (real[:STA], imag[:STA], real[STA:], imag[STA:])
        for quarter in range(4):
            piece = None
            for k in range(4):
                shift = (32 * (k - quarter)) % 128
                moved = pltpu.roll(parts[k], shift, 1) if shift else parts[k]
                piece = moved if piece is None else jnp.where(group == k, moved, piece)
            send_ref[4 * tile + quarter] = piece.astype(BF16)


def locate(pair_ref, tiles_ref, owner_ref, group):
    ends = 2 * PPD
    pairs = pair_ref[...]
    place = jnp.concatenate([diagonal_column(pairs[h : h + 1], PPD) for h in range(2)], axis=0)
    lanes = iota((ends, 128), 1)
    stations = tiles_ref[pl.ds(group, 1), :]
    found = jnp.zeros((ends, 128), I32)
    for c in range(3):
        found += jnp.where(place == lanes + 128 * c, stations[:, 128 * c : 128 * c + 128], 0)
    station = jnp.sum(found, axis=1, keepdims=True)
    found = jnp.zeros((ends, 128), I32)
    for c in range(32):
        found += jnp.where(station == lanes + 128 * c, owner_ref[c : c + 1, :], 0)
    owner = jnp.sum(found, axis=1, keepdims=True)
    found = jnp.zeros((ends, 128), I32)
    for c in range(32):
        ahead = (owner_ref[c : c + 1, :] == owner) & (lanes + 128 * c < station)
        found += jnp.where(ahead, 1, 0)
    rank = jnp.sum(found, axis=1, keepdims=True)
    part, member = lax.div(owner, NG), lax.rem(owner, NG)
    row = (lax.rem(part, NZ) * LAYER + lax.div(part, NZ) * NG + member) * STA + rank
    spread = jnp.where(iota((ends, 128), 0) == lanes, jnp.broadcast_to(row, (ends, 128)), 0)
    return jnp.sum(spread, axis=0, keepdims=True)


def table_angles(c8_ref, s8_ref, dc_ref, ds_ref, base_ref):
    shift = NFFT - MAXLAG
    sub, lane = iota((8, 128), 0), iota((8, 128), 1)
    fine = angle(sub * (lane + shift))
    base_ref[0] = jnp.cos(fine)
    base_ref[1] = jnp.sin(fine)
    coarse = angle(8 * iota((128, 128), 0) * (iota((128, 128), 1) + shift))
    c8_ref[...] = jnp.cos(coarse)
    s8_ref[...] = jnp.sin(coarse)
    for j in range(16):
        turn = angle(128 * j * sub)
        dc_ref[j] = jnp.cos(turn)
        ds_ref[j] = jnp.sin(turn)


def build_table(start, stop, table_ref, c8_ref, s8_ref, dc_ref, ds_ref, base_ref):
    def block(u, carry):
        c0, s0 = base_ref[0], base_ref[1]
        for h in range(2):
            base = []
            for q in range(2):
                v = 4 * u + 2 * h + q
                cv, sv = c8_ref[pl.ds(v, 1), :], s8_ref[pl.ds(v, 1), :]
                c, s = cv * c0 - sv * s0, sv * c0 + cv * s0
                base.append((c, s, -c, -s))
            for j in range(16):
                dc, ds = dc_ref[j], ds_ref[j]
                reals, imags = [], []
                for q in range(2):
                    c, s, nc, ns = base[q]
                    if q == 1 and j % 2 == 1:
                        c, s, nc, ns = nc, ns, c, s
                    reals.append(c * dc - s * ds)
                    imags.append(ns * dc + nc * ds)
                top = pl.multiple_of(64 * u + 16 * h, 16)
                low = pl.multiple_of(64 * u + 32 + 16 * h, 16)
                cols = slice(128 * j, 128 * j + 128)
                table_ref[pl.ds(top, 16), cols] = jnp.concatenate(reals, axis=0).astype(BF16)
                table_ref[pl.ds(low, 16), cols] = jnp.concatenate(imags, axis=0).astype(BF16)
        return carry

    lax.fori_loop(start, stop, block, 0)


def kernel(
    spec_hbm, station_hbm, window_hbm, owner_hbm, tiles_hbm, pair_hbm, out_ref,
    spec_ref, station_ref, window_ref, owner_ref, tiles_ref, pair_ref,
    send_ref, rows_ref, wide_ref, index_ref, place_ref, first_ref, second_ref, cross_ref, got_ref, left_ref, total_ref,
    table_ref, c8_ref, s8_ref, dc_ref, ds_ref, base_ref,
    piece_send, piece_recv, index_send, index_recv, cross_send, cross_recv, ring_send, ring_recv, load_sem, local_sem,
):
    group, member = lax.axis_index("pairs"), lax.axis_index("grp")
    x, z = lax.div(group, NZ), lax.rem(group, NZ)
    me = x * NG + member
    sources = (spec_hbm, station_hbm, window_hbm, owner_hbm, tiles_hbm, pair_hbm)
    targets = (spec_ref, station_ref, window_ref, owner_ref, tiles_ref, pair_ref)
    loads = [pltpu.make_async_copy(a, b, load_sem.at[n]) for n, (a, b) in enumerate(zip(sources, targets))]
    for load in loads:
        load.start()

    def device(along, across, layer):
        return (along * NZ + layer, across)

    def column(t):
        return lax.rem(x + jnp.where(t == 0, 2, jnp.where(t == 1, 1, jnp.where(t == 2, 3, 0))), NX)

    def across(m):
        return lax.rem(member + 2 * NG - 1 - m, NG)

    def each_peer(act):
        def one_column(t, carry):
            along = column(t)

            def one(m, c):
                act(along, across(m))
                return c

            return lax.fori_loop(0, jnp.where(t < NX - 1, NG, NG - 1), one, carry)

        lax.fori_loop(0, NX, one_column, 0)

    def layer_at(offset):
        return lax.rem(z + NZ + offset, NZ)

    def arrived(ref, sem):
        pltpu.make_async_remote_copy(
            src_ref=ref, dst_ref=ref, send_sem=piece_send, recv_sem=sem,
            device_id=device(x, member, layer_at(1)), device_id_type=MESH,
        ).wait_recv()

    def left(ref, sem):
        pltpu.make_async_remote_copy(
            src_ref=ref, dst_ref=ref, send_sem=sem, recv_sem=index_recv,
            device_id=device(x, member, layer_at(1)), device_id_type=MESH,
        ).wait_send()

    barrier = pltpu.get_barrier_semaphore()

    for offset in (2, -2, 1, -1):
        pl.semaphore_signal(barrier, inc=1, device_id=device(x, member, layer_at(offset)), device_id_type=MESH)
    each_peer(lambda a, m: pl.semaphore_signal(barrier, inc=1, device_id=device(a, m, z), device_id_type=MESH))

    for load in loads[:3]:
        load.wait()
    pack_rows(spec_ref, station_ref, window_ref, send_ref)
    rows_ref[z, me] = send_ref[me]
    for load in loads[3:]:
        load.wait()
    pl.semaphore_wait(barrier, LAYER - 1 + 4)

    def piece_copy(along, across):
        return pltpu.make_async_remote_copy(
            src_ref=send_ref.at[along * NG + across], dst_ref=rows_ref.at[z, me],
            send_sem=piece_send, recv_sem=piece_recv.at[lax.div(x, NX // HALVES)],
            device_id=device(along, across, z), device_id_type=MESH,
        )

    def index_copy(along, across):
        return pltpu.make_async_remote_copy(
            src_ref=index_ref.at[me], dst_ref=index_ref.at[me],
            send_sem=index_send, recv_sem=index_recv,
            device_id=device(along, across, z), device_id_type=MESH,
        )

    def cross_copy(along, across):
        return pltpu.make_async_remote_copy(
            src_ref=cross_ref.at[along * NG + across], dst_ref=got_ref.at[me],
            send_sem=cross_send, recv_sem=cross_recv.at[x],
            device_id=device(along, across, z), device_id_type=MESH,
        )

    each_peer(lambda a, m: piece_copy(a, m).start())
    index_ref[me] = locate(pair_ref, tiles_ref, owner_ref, group)
    table_angles(c8_ref, s8_ref, dc_ref, ds_ref, base_ref)
    each_peer(lambda a, m: index_copy(a, m).start())

    def table_part(start, stop):
        build_table(start, stop, table_ref, c8_ref, s8_ref, dc_ref, ds_ref, base_ref)

    def ring_copy(way, distance, s, chunk, step):
        part = pl.ds(PART * s, PART)
        return pltpu.make_async_remote_copy(
            src_ref=rows_ref.at[chunk, part], dst_ref=rows_ref.at[chunk, part],
            send_sem=ring_send, recv_sem=ring_recv.at[way, distance, s],
            device_id=device(x, member, layer_at(step if way == 0 else -step)), device_id_type=MESH,
        )

    def widen(chunk, s):
        start = pl.multiple_of((chunk * LAYER + s * PART) * STA, 128)
        rows = rows_ref[chunk, pl.ds(PART * s, PART)].astype(F32)
        wide_ref[pl.ds(start, PART * STA), :] = rows.reshape(PART * STA, 128)

    def chunk_of(way, distance):
        return lax.rem(z + NZ - distance, NZ) if way == 0 else lax.rem(z + distance, NZ)

    def half(k):
        return lax.rem(lax.div(x, 2) + k, HALVES)

    def start_half(k, carry):
        s = half(k)

        @pl.when(k == 0)
        def _():
            arrived(rows_ref.at[z, pl.ds(PART * s, PART - 1)], piece_recv.at[s])

        @pl.when(k == 1)
        def _():
            arrived(rows_ref.at[z, pl.ds(PART * s, PART)], piece_recv.at[s])

        for way in range(2):
            ring_copy(way, 2, s, z, 2).start()
            ring_copy(way, 1, s, z, 1).start()
        return carry

    lax.fori_loop(0, HALVES, start_half, 0)
    for s in range(HALVES):
        widen(z, s)
    table_part(0, 6)

    arrived(index_ref.at[pl.ds(0, LAYER - 1)], index_recv)
    to_scalar = pltpu.make_async_copy(index_ref, place_ref, local_sem)
    to_scalar.start()

    def stop(i, carry):
        distance = 2 * i + 2

        def one_half(k, c):
            s = half(k)
            for way in range(2):
                chunk = chunk_of(way, distance)

                @pl.when((distance < 8) | (k == way))
                def _():
                    ring_copy(way, distance, s, chunk, 2).wait_recv()

                @pl.when((distance < 6) | ((distance == 6) & (k == way)))
                def _():
                    ring_copy(way, distance + 2, s, chunk, 2).start()

                @pl.when(distance < 8)
                def _():
                    ring_copy(way, distance + 1, s, chunk, 1).start()

                @pl.when((distance < 8) | (k == way))
                def _():
                    widen(chunk, s)
            return c

        lax.fori_loop(0, HALVES, one_half, 0)

        def odd_half(k, c):
            s = half(k)
            for way in range(2):
                chunk = chunk_of(way, distance - 1)
                ring_copy(way, distance - 1, s, chunk, 1).wait_recv()
                widen(chunk, s)
            return c

        lax.fori_loop(0, HALVES, odd_half, 0)

        @pl.when(distance < 8)
        def _():
            table_part(6 + 9 * i, jnp.minimum(15 + 9 * i, LAYER))

        return carry

    lax.fori_loop(0, 4, stop, 0)
    to_scalar.wait()

    lane = iota((PPD, 128), 1)
    odd = lax.rem(lax.div(lane, 32), 2) == 1
    low = iota((PPD // 2, 128), 1) < 64

    first_ref[...] = jnp.zeros((PPD, 128), F32)
    second_ref[...] = jnp.zeros((PPD, 128), F32)

    def correlate(j, carry):
        a, b = first_ref[...], second_ref[...]
        last_a, last_m, before_a, before_m = carry
        turn = jnp.minimum(j, LAYER - 1)
        now_a, now_m = column(lax.div(turn, NG)), across(lax.rem(turn, NG))
        number = now_a * NG + now_m
        for k in range(PPD):
            first = place_ref[number, 0, k] & (TOTAL - 1)
            second = place_ref[number, 0, PPD + k] & (TOTAL - 1)
            first_ref[k : k + 1, :] = wide_ref[pl.ds(first, 1), :]
            second_ref[k : k + 1, :] = wide_ref[pl.ds(second, 1), :]
        turned = jnp.where(odd, pltpu.roll(b, 32, 1), -pltpu.roll(b, 96, 1))
        real, imag = a * b, a * turned
        real = real + pltpu.roll(real, 64, 1)
        real = real + pltpu.roll(real, 32, 1)
        imag = imag + pltpu.roll(imag, 64, 1)
        imag = imag + pltpu.roll(imag, 32, 1)
        both = jnp.where(odd, imag, real)
        packed = jnp.where(low, both[: PPD // 2], both[PPD // 2 :])
        cross_ref[last_a * NG + last_m] = packed.astype(BF16).reshape(3, 8, 128)

        @pl.when(j > 1)
        def _():
            cross_copy(before_a, before_m).start()

        return now_a, now_m, last_a, last_m

    start = (column(0), across(0), column(0), across(0))
    lax.fori_loop(0, LAYER + 1, correlate, start)
    got_ref[me] = cross_ref[me]

    scale = 1.0 / math.sqrt(HALF * W)
    depth = 2 * HALF // NX

    def product(t, carry):
        along = column(t)
        base = along * NG

        @pl.when(t < NX - 1)
        def _():
            arrived(got_ref.at[pl.ds(base, NG)], cross_recv.at[along])

        @pl.when(t == NX - 1)
        def _():
            arrived(got_ref.at[pl.ds(base, NG - 1)], cross_recv.at[along])

        for i in range(NG // 2):
            one = got_ref[base + 2 * i].astype(F32).reshape(PPD // 2, 128)
            two = got_ref[base + 2 * i + 1].astype(F32).reshape(PPD // 2, 128)
            top = jnp.where(low, one, pltpu.roll(two, 64, 1))
            bottom = jnp.where(low, pltpu.roll(one, 64, 1), two)
            left_ref[:, 128 * i : 128 * i + 128] = jnp.concatenate([top, bottom], axis=0).astype(BF16)
        rows = pl.ds(pl.multiple_of(base * (depth // NG), depth), depth)

        def columns(n, c):
            cols = pl.ds(pl.multiple_of(256 * n, 256), 256)
            total_ref[:, cols] += jnp.dot(left_ref[...], table_ref[rows, cols], preferred_element_type=F32)
            return c

        lax.fori_loop(0, 8, columns, 0)
        return carry

    total_ref[...] = jnp.zeros((PPD, NFFT), F32)
    lax.fori_loop(0, NX, product, 0)
    out_ref[...] = total_ref[:, :LAGS] * scale

    left(send_ref.at[pl.ds(0, LAYER - 1)], piece_send)
    left(index_ref.at[pl.ds(0, LAYER - 1)], index_send)
    left(cross_ref.at[pl.ds(0, LAYER - 1)], cross_send)
    left(rows_ref.at[pl.ds(0, NZ - 1)], ring_send)


def on_device(spectra, row_station, row_window, station_owner, tile_stations, pair_index):
    vmem = pl.BlockSpec(memory_space=pltpu.VMEM)
    dma = pltpu.SemaphoreType.DMA
    result = pl.pallas_call(
        kernel,
        out_shape=jax.ShapeDtypeStruct((PPD, LAGS), F32),
        in_specs=[pl.BlockSpec(memory_space=pl.ANY)] * 6,
        out_specs=vmem,
        scratch_shapes=[
            pltpu.VMEM((2 * STA, NFFT), BF16),
            pltpu.VMEM((1, 2 * STA), I32),
            pltpu.VMEM((1, 2 * STA), I32),
            pltpu.VMEM((32, 128), I32),
            pltpu.VMEM((NX * NZ, NG * PPD), I32),
            pltpu.VMEM((2, PPD), I32),
            pltpu.VMEM((LAYER, STA, 128), BF16),
            pltpu.VMEM((NZ, LAYER, STA, 128), BF16),
            pltpu.VMEM((TOTAL, 128), F32),
            pltpu.VMEM((LAYER, 1, 128), I32),
            pltpu.SMEM((LAYER, 1, 128), I32),
            pltpu.VMEM((PPD, 128), F32),
            pltpu.VMEM((PPD, 128), F32),
            pltpu.VMEM((LAYER, 3, 8, 128), BF16),
            pltpu.VMEM((LAYER, 3, 8, 128), BF16),
            pltpu.VMEM((PPD, NFFT // NX), BF16),
            pltpu.VMEM((PPD, NFFT), F32),
            pltpu.VMEM((NFFT, NFFT), BF16),
            pltpu.VMEM((128, 128), F32),
            pltpu.VMEM((128, 128), F32),
            pltpu.VMEM((16, 8, 128), F32),
            pltpu.VMEM((16, 8, 128), F32),
            pltpu.VMEM((2, 8, 128), F32),
            dma,
            dma((HALVES,)),
            dma,
            dma,
            dma,
            dma((NX,)),
            dma,
            dma((2, 9, HALVES)),
            dma((6,)),
            dma,
        ],
        compiler_params=pltpu.CompilerParams(
            collective_id=0, has_side_effects=True, vmem_limit_bytes=62 * 1024 * 1024
        ),
    )(
        spectra.reshape(2 * STA, NFFT),
        row_station.reshape(1, 2 * STA),
        row_window.reshape(1, 2 * STA),
        station_owner.reshape(32, 128),
        tile_stations,
        pair_index.reshape(2, PPD),
    )
    return result.reshape(1, 1, PPD, LAGS)


def solution(mesh):
    placed = (
        P(("pairs", "grp"), None, None),
        P(("pairs", "grp")),
        P(("pairs", "grp")),
        P(),
        P(),
        P("pairs", "grp", None, None),
    )
    return jax.shard_map(
        on_device,
        mesh=mesh,
        in_specs=placed,
        out_specs=P("pairs", "grp", None, None),
        check_vma=False,
    )
```

```python
import math

import jax
import jax.numpy as jnp
from jax import lax
from jax.experimental import pallas as pl
from jax.experimental.pallas import tpu as pltpu
from jax.sharding import PartitionSpec as P

MESH = pl.DeviceIdType.MESH
W = 2
NFFT = 2048
HALF = 1024
MAXLAG = 1000
LAGS = 2001
EPS = 1e-06
NX = 4
NZ = 16
NG = 8
LAYER = NX * NG
STA = 8
PPD = 48
TOTAL = NZ * LAYER * STA
HALVES = 2
PART = LAYER // HALVES
STEP = 2.0 * math.pi / NFFT
F32 = jnp.float32
I32 = jnp.int32
BF16 = jnp.bfloat16


def iota(shape, axis):
    return lax.broadcasted_iota(I32, shape, axis)


def angle(steps):
    return lax.rem(steps, NFFT).astype(F32) * STEP


def diagonal_column(row, size):
    same = iota((size, size), 0) == iota((size, size), 1)
    return jnp.sum(jnp.where(same, jnp.broadcast_to(row, (size, size)), 0), axis=1, keepdims=True)


def pack_rows(spec_ref, station_ref, window_ref, send_ref):
    station = station_ref[...]
    column = diagonal_column(station, 2 * STA)
    ahead = jnp.sum(jnp.where(column < station, 1, 0), axis=0, keepdims=True)
    place = window_ref[...] * STA + lax.div(ahead, W)
    order = jnp.where(iota((2 * STA, 2 * STA), 0) == place, 1.0, 0.0).astype(BF16)
    group = lax.div(iota((STA, 128), 1), 32)
    for tile in range(8):
        real = spec_ref[:, 128 * tile : 128 * tile + 128].astype(F32)
        imag = spec_ref[:, HALF + 128 * tile : HALF + 128 * tile + 128].astype(F32)
        power = jnp.sum(real * real + imag * imag, axis=1, keepdims=True) * (1.0 / 128)
        scale = lax.rsqrt(power + EPS)
        real = jnp.dot(order, (real * scale).astype(BF16), preferred_element_type=F32)
        imag = jnp.dot(order, (imag * scale).astype(BF16), preferred_element_type=F32)
        parts = (real[:STA], real[STA:], imag[:STA], imag[STA:])
        for quarter in range(4):
            piece = None
            for k in range(4):
                shift = (32 * (k - quarter)) % 128
                moved = pltpu.roll(parts[k], shift, 1) if shift else parts[k]
                piece = moved if piece is None else jnp.where(group == k, moved, piece)
            send_ref[4 * tile + quarter] = piece.astype(BF16)


def locate(pair_ref, tiles_ref, owner_ref, group):
    ends = 2 * PPD
    pairs = pair_ref[...]
    place = jnp.concatenate([diagonal_column(pairs[h : h + 1], PPD) for h in range(2)], axis=0)
    lanes = iota((ends, 128), 1)
    stations = tiles_ref[pl.ds(group, 1), :]
    found = jnp.zeros((ends, 128), I32)
    for c in range(3):
        found += jnp.where(place == lanes + 128 * c, stations[:, 128 * c : 128 * c + 128], 0)
    station = jnp.sum(found, axis=1, keepdims=True)
    found = jnp.zeros((ends, 128), I32)
    for c in range(32):
        found += jnp.where(station == lanes + 128 * c, owner_ref[c : c + 1, :], 0)
    owner = jnp.sum(found, axis=1, keepdims=True)
    found = jnp.zeros((ends, 128), I32)
    for c in range(32):
        ahead = (owner_ref[c : c + 1, :] == owner) & (lanes + 128 * c < station)
        found += jnp.where(ahead, 1, 0)
    rank = jnp.sum(found, axis=1, keepdims=True)
    part, member = lax.div(owner, NG), lax.rem(owner, NG)
    row = (lax.rem(part, NZ) * LAYER + lax.div(part, NZ) * NG + member) * STA + rank
    spread = jnp.where(iota((ends, 128), 0) == lanes, jnp.broadcast_to(row, (ends, 128)), 0)
    return jnp.sum(spread, axis=0, keepdims=True)


def table_angles(c8_ref, s8_ref, dc_ref, ds_ref, base_ref):
    shift = NFFT - MAXLAG
    sub, lane = iota((8, 128), 0), iota((8, 128), 1)
    fine = angle(sub * (lane + shift))
    base_ref[0] = jnp.cos(fine)
    base_ref[1] = jnp.sin(fine)
    coarse = angle(8 * iota((128, 128), 0) * (iota((128, 128), 1) + shift))
    c8_ref[...] = jnp.cos(coarse)
    s8_ref[...] = jnp.sin(coarse)
    for j in range(16):
        turn = angle(128 * j * sub)
        dc_ref[j] = jnp.cos(turn)
        ds_ref[j] = jnp.sin(turn)


def build_table(start, stop, table_ref, c8_ref, s8_ref, dc_ref, ds_ref, base_ref):
    def block(u, carry):
        c0, s0 = base_ref[0], base_ref[1]
        for h in range(2):
            base = []
            for q in range(2):
                v = 4 * u + 2 * h + q
                cv, sv = c8_ref[pl.ds(v, 1), :], s8_ref[pl.ds(v, 1), :]
                c, s = cv * c0 - sv * s0, sv * c0 + cv * s0
                base.append((c, s, -c, -s))
            for j in range(16):
                dc, ds = dc_ref[j], ds_ref[j]
                reals, imags = [], []
                for q in range(2):
                    c, s, nc, ns = base[q]
                    if q == 1 and j % 2 == 1:
                        c, s, nc, ns = nc, ns, c, s
                    reals.append(c * dc - s * ds)
                    imags.append(ns * dc + nc * ds)
                top = pl.multiple_of(64 * u + 16 * h, 16)
                low = pl.multiple_of(64 * u + 32 + 16 * h, 16)
                cols = slice(128 * j, 128 * j + 128)
                table_ref[pl.ds(top, 16), cols] = jnp.concatenate(reals, axis=0).astype(BF16)
                table_ref[pl.ds(low, 16), cols] = jnp.concatenate(imags, axis=0).astype(BF16)
        return carry

    lax.fori_loop(start, stop, block, 0)


def kernel(
    spec_hbm, station_hbm, window_hbm, owner_hbm, tiles_hbm, pair_hbm, out_ref,
    spec_ref, station_ref, window_ref, owner_ref, tiles_ref, pair_ref,
    send_ref, rows_ref, wide_ref, index_ref, place_ref, first_ref, second_ref, cross_ref, got_ref, left_ref, total_ref,
    table_ref, c8_ref, s8_ref, dc_ref, ds_ref, base_ref,
    piece_send, piece_recv, index_send, index_recv, cross_send, cross_recv, ring_send, ring_recv, load_sem, local_sem,
):
    group, member = lax.axis_index("pairs"), lax.axis_index("grp")
    x, z = lax.div(group, NZ), lax.rem(group, NZ)
    me = x * NG + member
    sources = (spec_hbm, station_hbm, window_hbm, owner_hbm, tiles_hbm, pair_hbm)
    targets = (spec_ref, station_ref, window_ref, owner_ref, tiles_ref, pair_ref)
    loads = [pltpu.make_async_copy(a, b, load_sem.at[n]) for n, (a, b) in enumerate(zip(sources, targets))]
    for load in loads:
        load.start()

    def device(along, across, layer):
        return (along * NZ + layer, across)

    def column(t):
        return lax.rem(x + jnp.where(t == 0, 2, jnp.where(t == 1, 1, jnp.where(t == 2, 3, 0))), NX)

    def across(m):
        return lax.rem(member + 2 * NG - 1 - m, NG)

    def each_peer(act):
        def one_column(t, carry):
            along = column(t)

            def one(m, c):
                act(along, across(m))
                return c

            return lax.fori_loop(0, jnp.where(t < NX - 1, NG, NG - 1), one, carry)

        lax.fori_loop(0, NX, one_column, 0)

    def layer_at(offset):
        return lax.rem(z + NZ + offset, NZ)

    def arrived(ref, sem):
        pltpu.make_async_remote_copy(
            src_ref=ref, dst_ref=ref, send_sem=piece_send, recv_sem=sem,
            device_id=device(x, member, layer_at(1)), device_id_type=MESH,
        ).wait_recv()

    def left(ref, sem):
        pltpu.make_async_remote_copy(
            src_ref=ref, dst_ref=ref, send_sem=sem, recv_sem=index_recv,
            device_id=device(x, member, layer_at(1)), device_id_type=MESH,
        ).wait_send()

    barrier = pltpu.get_barrier_semaphore()

    for offset in (2, -2, 1, -1):
        pl.semaphore_signal(barrier, inc=1, device_id=device(x, member, layer_at(offset)), device_id_type=MESH)
    each_peer(lambda a, m: pl.semaphore_signal(barrier, inc=1, device_id=device(a, m, z), device_id_type=MESH))

    for load in loads[:3]:
        load.wait()
    pack_rows(spec_ref, station_ref, window_ref, send_ref)
    rows_ref[z, me] = send_ref[me]
    for load in loads[3:]:
        load.wait()
    pl.semaphore_wait(barrier, LAYER - 1 + 4)

    def piece_copy(along, across):
        return pltpu.make_async_remote_copy(
            src_ref=send_ref.at[along * NG + across], dst_ref=rows_ref.at[z, me],
            send_sem=piece_send, recv_sem=piece_recv.at[lax.div(x, NX // HALVES)],
            device_id=device(along, across, z), device_id_type=MESH,
        )

    def index_copy(along, across):
        return pltpu.make_async_remote_copy(
            src_ref=index_ref.at[me], dst_ref=index_ref.at[me],
            send_sem=index_send, recv_sem=index_recv,
            device_id=device(along, across, z), device_id_type=MESH,
        )

    def cross_copy(along, across):
        return pltpu.make_async_remote_copy(
            src_ref=cross_ref.at[along * NG + across], dst_ref=got_ref.at[me],
            send_sem=cross_send, recv_sem=cross_recv.at[x],
            device_id=device(along, across, z), device_id_type=MESH,
        )

    each_peer(lambda a, m: piece_copy(a, m).start())
    index_ref[me] = locate(pair_ref, tiles_ref, owner_ref, group)
    table_angles(c8_ref, s8_ref, dc_ref, ds_ref, base_ref)
    each_peer(lambda a, m: index_copy(a, m).start())

    def table_part(start, stop):
        build_table(start, stop, table_ref, c8_ref, s8_ref, dc_ref, ds_ref, base_ref)

    def ring_copy(way, distance, s, chunk, step):
        part = pl.ds(PART * s, PART)
        return pltpu.make_async_remote_copy(
            src_ref=rows_ref.at[chunk, part], dst_ref=rows_ref.at[chunk, part],
            send_sem=ring_send, recv_sem=ring_recv.at[way, distance, s],
            device_id=device(x, member, layer_at(step if way == 0 else -step)), device_id_type=MESH,
        )

    def widen(chunk, s):
        start = pl.multiple_of((chunk * LAYER + s * PART) * STA, 128)
        rows = rows_ref[chunk, pl.ds(PART * s, PART)].astype(F32)
        wide_ref[pl.ds(start, PART * STA), :] = rows.reshape(PART * STA, 128)

    def chunk_of(way, distance):
        return lax.rem(z + NZ - distance, NZ) if way == 0 else lax.rem(z + distance, NZ)

    def half(k):
        return lax.rem(lax.div(x, 2) + k, HALVES)

    def start_half(k, carry):
        s = half(k)

        @pl.when(k == 0)
        def _():
            arrived(rows_ref.at[z, pl.ds(PART * s, PART - 1)], piece_recv.at[s])

        @pl.when(k == 1)
        def _():
            arrived(rows_ref.at[z, pl.ds(PART * s, PART)], piece_recv.at[s])

        for way in range(2):
            ring_copy(way, 2, s, z, 2).start()
            ring_copy(way, 1, s, z, 1).start()
        return carry

    lax.fori_loop(0, HALVES, start_half, 0)
    for s in range(HALVES):
        widen(z, s)
    table_part(0, 6)

    arrived(index_ref.at[pl.ds(0, LAYER - 1)], index_recv)
    to_scalar = pltpu.make_async_copy(index_ref, place_ref, local_sem)
    to_scalar.start()

    def stop(i, carry):
        distance = 2 * i + 2

        def one_half(k, c):
            s = half(k)
            for way in range(2):
                chunk = chunk_of(way, distance)

                @pl.when((distance < 8) | (k == way))
                def _():
                    ring_copy(way, distance, s, chunk, 2).wait_recv()

                @pl.when((distance < 6) | ((distance == 6) & (k == way)))
                def _():
                    ring_copy(way, distance + 2, s, chunk, 2).start()

                @pl.when(distance < 8)
                def _():
                    ring_copy(way, distance + 1, s, chunk, 1).start()

                @pl.when((distance < 8) | (k == way))
                def _():
                    widen(chunk, s)
            return c

        lax.fori_loop(0, HALVES, one_half, 0)

        def odd_half(k, c):
            s = half(k)
            for way in range(2):
                chunk = chunk_of(way, distance - 1)
                ring_copy(way, distance - 1, s, chunk, 1).wait_recv()
                widen(chunk, s)
            return c

        lax.fori_loop(0, HALVES, odd_half, 0)

        @pl.when(distance < 8)
        def _():
            table_part(6 + 9 * i, jnp.minimum(15 + 9 * i, LAYER))

        return carry

    lax.fori_loop(0, 4, stop, 0)
    to_scalar.wait()

    lane = iota((PPD, 128), 1)
    odd = lax.rem(lax.div(lane, 32), 2) == 1
    low = iota((PPD // 2, 128), 1) < 64
    sign = jnp.where(lane < 64, -1.0, 1.0)

    first_ref[...] = jnp.zeros((PPD, 128), F32)
    second_ref[...] = jnp.zeros((PPD, 128), F32)

    def correlate(j, carry):
        a, b = first_ref[...], second_ref[...]
        last_a, last_m, before_a, before_m = carry
        turn = jnp.minimum(j, LAYER - 1)
        now_a, now_m = column(lax.div(turn, NG)), across(lax.rem(turn, NG))
        number = now_a * NG + now_m
        for k in range(PPD):
            first = place_ref[number, 0, k] & (TOTAL - 1)
            second = place_ref[number, 0, PPD + k] & (TOTAL - 1)
            first_ref[k : k + 1, :] = wide_ref[pl.ds(first, 1), :]
            second_ref[k : k + 1, :] = wide_ref[pl.ds(second, 1), :]
        real, imag = a * b, a * (pltpu.roll(b, 64, 1) * sign)
        kept, moved = jnp.where(odd, imag, real), jnp.where(odd, real, imag)
        both = kept + pltpu.roll(moved, 96, 1)
        both = both + pltpu.roll(both, 64, 1)
        packed = jnp.where(low, both[: PPD // 2], both[PPD // 2 :])
        cross_ref[last_a * NG + last_m] = packed.astype(BF16).reshape(3, 8, 128)

        @pl.when(j > 1)
        def _():
            cross_copy(before_a, before_m).start()

        return now_a, now_m, last_a, last_m

    start = (column(0), across(0), column(0), across(0))
    lax.fori_loop(0, LAYER + 1, correlate, start)
    got_ref[me] = cross_ref[me]

    scale = 1.0 / math.sqrt(HALF * W)
    depth = 2 * HALF // NX

    def product(t, carry):
        along = column(t)
        base = along * NG

        @pl.when(t < NX - 1)
        def _():
            arrived(got_ref.at[pl.ds(base, NG)], cross_recv.at[along])

        @pl.when(t == NX - 1)
        def _():
            arrived(got_ref.at[pl.ds(base, NG - 1)], cross_recv.at[along])

        for i in range(NG // 2):
            one = got_ref[base + 2 * i].astype(F32).reshape(PPD // 2, 128)
            two = got_ref[base + 2 * i + 1].astype(F32).reshape(PPD // 2, 128)
            top = jnp.where(low, one, pltpu.roll(two, 64, 1))
            bottom = jnp.where(low, pltpu.roll(one, 64, 1), two)
            left_ref[:, 128 * i : 128 * i + 128] = jnp.concatenate([top, bottom], axis=0).astype(BF16)
        rows = pl.ds(pl.multiple_of(base * (depth // NG), depth), depth)

        def columns(n, c):
            cols = pl.ds(pl.multiple_of(256 * n, 256), 256)
            total_ref[:, cols] += jnp.dot(left_ref[...], table_ref[rows, cols], preferred_element_type=F32)
            return c

        lax.fori_loop(0, 8, columns, 0)
        return carry

    total_ref[...] = jnp.zeros((PPD, NFFT), F32)
    lax.fori_loop(0, NX, product, 0)
    out_ref[...] = total_ref[:, :LAGS] * scale

    left(send_ref.at[pl.ds(0, LAYER - 1)], piece_send)
    left(index_ref.at[pl.ds(0, LAYER - 1)], index_send)
    left(cross_ref.at[pl.ds(0, LAYER - 1)], cross_send)
    left(rows_ref.at[pl.ds(0, NZ - 1)], ring_send)


def on_device(spectra, row_station, row_window, station_owner, tile_stations, pair_index):
    vmem = pl.BlockSpec(memory_space=pltpu.VMEM)
    dma = pltpu.SemaphoreType.DMA
    result = pl.pallas_call(
        kernel,
        out_shape=jax.ShapeDtypeStruct((PPD, LAGS), F32),
        in_specs=[pl.BlockSpec(memory_space=pltpu.HBM)] * 6,
        out_specs=vmem,
        scratch_shapes=[
            pltpu.VMEM((2 * STA, NFFT), BF16),
            pltpu.VMEM((1, 2 * STA), I32),
            pltpu.VMEM((1, 2 * STA), I32),
            pltpu.VMEM((32, 128), I32),
            pltpu.VMEM((NX * NZ, NG * PPD), I32),
            pltpu.VMEM((2, PPD), I32),
            pltpu.VMEM((LAYER, STA, 128), BF16),
            pltpu.VMEM((NZ, LAYER, STA, 128), BF16),
            pltpu.VMEM((TOTAL, 128), F32),
            pltpu.VMEM((LAYER, 1, 128), I32),
            pltpu.SMEM((LAYER, 1, 128), I32),
            pltpu.VMEM((PPD, 128), F32),
            pltpu.VMEM((PPD, 128), F32),
            pltpu.VMEM((LAYER, 3, 8, 128), BF16),
            pltpu.VMEM((LAYER, 3, 8, 128), BF16),
            pltpu.VMEM((PPD, NFFT // NX), BF16),
            pltpu.VMEM((PPD, NFFT), F32),
            pltpu.VMEM((NFFT, NFFT), BF16),
            pltpu.VMEM((128, 128), F32),
            pltpu.VMEM((128, 128), F32),
            pltpu.VMEM((16, 8, 128), F32),
            pltpu.VMEM((16, 8, 128), F32),
            pltpu.VMEM((2, 8, 128), F32),
            dma,
            dma((HALVES,)),
            dma,
            dma,
            dma,
            dma((NX,)),
            dma,
            dma((2, 9, HALVES)),
            dma((6,)),
            dma,
        ],
        compiler_params=pltpu.CompilerParams(
            collective_id=0, has_side_effects=True, vmem_limit_bytes=48 * 1024 * 1024
        ),
    )(*[pltpu.with_memory_space_constraint(v, pltpu.HBM) for v in (
        spectra.reshape(2 * STA, NFFT),
        row_station.reshape(1, 2 * STA),
        row_window.reshape(1, 2 * STA),
        station_owner.reshape(32, 128),
        tile_stations,
        pair_index.reshape(2, PPD),
    )])
    return result.reshape(1, 1, PPD, LAGS)


def solution(mesh):
    placed = (
        P(("pairs", "grp"), None, None),
        P(("pairs", "grp")),
        P(("pairs", "grp")),
        P(),
        P(),
        P("pairs", "grp", None, None),
    )
    return jax.shard_map(
        on_device,
        mesh=mesh,
        in_specs=placed,
        out_specs=P("pairs", "grp", None, None),
        check_vma=False,
    )
```

```python
import math

import jax
import jax.numpy as jnp
from jax import lax
from jax.experimental import pallas as pl
from jax.experimental.pallas import tpu as pltpu
from jax.sharding import PartitionSpec as P

MESH = pl.DeviceIdType.MESH
W = 2
NFFT = 2048
HALF = 1024
MAXLAG = 1000
LAGS = 2001
EPS = 1e-06
NX = 4
NZ = 16
NG = 8
LAYER = NX * NG
STA = 8
PPD = 48
TOTAL = NZ * LAYER * STA
HALVES = 2
PART = LAYER // HALVES
STEP = 2.0 * math.pi / NFFT
F32 = jnp.float32
I32 = jnp.int32
BF16 = jnp.bfloat16


def iota(shape, axis):
    return lax.broadcasted_iota(I32, shape, axis)


def angle(steps):
    return lax.rem(steps, NFFT).astype(F32) * STEP


def diagonal_column(row, size):
    same = iota((size, size), 0) == iota((size, size), 1)
    return jnp.sum(jnp.where(same, jnp.broadcast_to(row, (size, size)), 0), axis=1, keepdims=True)


def pack_rows(spec_ref, station_ref, window_ref, send_ref):
    station = station_ref[...]
    column = diagonal_column(station, 2 * STA)
    ahead = jnp.sum(jnp.where(column < station, 1, 0), axis=0, keepdims=True)
    place = window_ref[...] * STA + lax.div(ahead, W)
    order = jnp.where(iota((2 * STA, 2 * STA), 0) == place, 1.0, 0.0).astype(BF16)
    group = lax.div(iota((STA, 128), 1), 32)
    for tile in range(8):
        real = spec_ref[:, 128 * tile : 128 * tile + 128].astype(F32)
        imag = spec_ref[:, HALF + 128 * tile : HALF + 128 * tile + 128].astype(F32)
        power = jnp.sum(real * real + imag * imag, axis=1, keepdims=True) * (1.0 / 128)
        scale = lax.rsqrt(power + EPS)
        real = jnp.dot(order, (real * scale).astype(BF16), preferred_element_type=F32)
        imag = jnp.dot(order, (imag * scale).astype(BF16), preferred_element_type=F32)
        parts = (real[:STA], real[STA:], imag[:STA], imag[STA:])
        for quarter in range(4):
            piece = None
            for k in range(4):
                shift = (32 * (k - quarter)) % 128
                moved = pltpu.roll(parts[k], shift, 1) if shift else parts[k]
                piece = moved if piece is None else jnp.where(group == k, moved, piece)
            send_ref[4 * tile + quarter] = piece.astype(BF16)


def locate(pair_ref, tiles_ref, owner_ref, group):
    ends = 2 * PPD
    pairs = pair_ref[...]
    place = jnp.concatenate([diagonal_column(pairs[h : h + 1], PPD) for h in range(2)], axis=0)
    lanes = iota((ends, 128), 1)
    stations = tiles_ref[pl.ds(group, 1), :]
    found = jnp.zeros((ends, 128), I32)
    for c in range(3):
        found += jnp.where(place == lanes + 128 * c, stations[:, 128 * c : 128 * c + 128], 0)
    station = jnp.sum(found, axis=1, keepdims=True)
    found = jnp.zeros((ends, 128), I32)
    for c in range(32):
        found += jnp.where(station == lanes + 128 * c, owner_ref[c : c + 1, :], 0)
    owner = jnp.sum(found, axis=1, keepdims=True)
    found = jnp.zeros((ends, 128), I32)
    for c in range(32):
        ahead = (owner_ref[c : c + 1, :] == owner) & (lanes + 128 * c < station)
        found += jnp.where(ahead, 1, 0)
    rank = jnp.sum(found, axis=1, keepdims=True)
    part, member = lax.div(owner, NG), lax.rem(owner, NG)
    row = (lax.rem(part, NZ) * LAYER + lax.div(part, NZ) * NG + member) * STA + rank
    spread = jnp.where(iota((ends, 128), 0) == lanes, jnp.broadcast_to(row, (ends, 128)), 0)
    return jnp.sum(spread, axis=0, keepdims=True)


def table_angles(c8_ref, s8_ref, dc_ref, ds_ref, base_ref):
    shift = NFFT - MAXLAG
    sub, lane = iota((8, 128), 0), iota((8, 128), 1)
    fine = angle(sub * (lane + shift))
    base_ref[0] = jnp.cos(fine)
    base_ref[1] = jnp.sin(fine)
    coarse = angle(8 * iota((128, 128), 0) * (iota((128, 128), 1) + shift))
    c8_ref[...] = jnp.cos(coarse)
    s8_ref[...] = jnp.sin(coarse)
    for j in range(16):
        turn = angle(128 * j * sub)
        dc_ref[j] = jnp.cos(turn)
        ds_ref[j] = jnp.sin(turn)


def build_table(start, stop, table_ref, c8_ref, s8_ref, dc_ref, ds_ref, base_ref):
    def block(u, carry):
        c0, s0 = base_ref[0], base_ref[1]
        for h in range(2):
            base = []
            for q in range(2):
                v = 4 * u + 2 * h + q
                cv, sv = c8_ref[pl.ds(v, 1), :], s8_ref[pl.ds(v, 1), :]
                c, s = cv * c0 - sv * s0, sv * c0 + cv * s0
                base.append((c, s, -c, -s))
            for j in range(16):
                dc, ds = dc_ref[j], ds_ref[j]
                reals, imags = [], []
                for q in range(2):
                    c, s, nc, ns = base[q]
                    if q == 1 and j % 2 == 1:
                        c, s, nc, ns = nc, ns, c, s
                    reals.append(c * dc - s * ds)
                    imags.append(ns * dc + nc * ds)
                top = pl.multiple_of(64 * u + 16 * h, 16)
                low = pl.multiple_of(64 * u + 32 + 16 * h, 16)
                cols = slice(128 * j, 128 * j + 128)
                table_ref[pl.ds(top, 16), cols] = jnp.concatenate(reals, axis=0).astype(BF16)
                table_ref[pl.ds(low, 16), cols] = jnp.concatenate(imags, axis=0).astype(BF16)
        return carry

    lax.fori_loop(start, stop, block, 0)


def kernel(
    spec_hbm, station_hbm, window_hbm, owner_hbm, tiles_hbm, pair_hbm, out_ref,
    spec_ref, station_ref, window_ref, owner_ref, tiles_ref, pair_ref,
    send_ref, rows_ref, wide_ref, index_ref, place_ref, first_ref, second_ref, cross_ref, got_ref, left_ref, total_ref,
    table_ref, c8_ref, s8_ref, dc_ref, ds_ref, base_ref,
    piece_send, piece_recv, index_send, index_recv, cross_send, cross_recv, ring_send, ring_recv, load_sem, local_sem,
):
    group, member = lax.axis_index("pairs"), lax.axis_index("grp")
    x, z = lax.div(group, NZ), lax.rem(group, NZ)
    me = x * NG + member
    sources = (spec_hbm, station_hbm, window_hbm, owner_hbm, tiles_hbm, pair_hbm)
    targets = (spec_ref, station_ref, window_ref, owner_ref, tiles_ref, pair_ref)
    loads = [pltpu.make_async_copy(a, b, load_sem.at[n]) for n, (a, b) in enumerate(zip(sources, targets))]
    for load in loads:
        load.start()

    def device(along, across, layer):
        return (along * NZ + layer, across)

    def column(t):
        return lax.rem(x + jnp.where(t == 0, 2, jnp.where(t == 1, 1, jnp.where(t == 2, 3, 0))), NX)

    def across(m):
        return lax.rem(member + 2 * NG - 1 - m, NG)

    def each_peer(act):
        def one_column(t, carry):
            along = column(t)

            def one(m, c):
                act(along, across(m))
                return c

            return lax.fori_loop(0, jnp.where(t < NX - 1, NG, NG - 1), one, carry)

        lax.fori_loop(0, NX, one_column, 0)

    def layer_at(offset):
        return lax.rem(z + NZ + offset, NZ)

    def arrived(ref, sem):
        pltpu.make_async_remote_copy(
            src_ref=ref, dst_ref=ref, send_sem=piece_send, recv_sem=sem,
            device_id=device(x, member, layer_at(1)), device_id_type=MESH,
        ).wait_recv()

    def left(ref, sem):
        pltpu.make_async_remote_copy(
            src_ref=ref, dst_ref=ref, send_sem=sem, recv_sem=index_recv,
            device_id=device(x, member, layer_at(1)), device_id_type=MESH,
        ).wait_send()

    barrier = pltpu.get_barrier_semaphore()

    for offset in (2, -2, 1, -1):
        pl.semaphore_signal(barrier, inc=1, device_id=device(x, member, layer_at(offset)), device_id_type=MESH)
    each_peer(lambda a, m: pl.semaphore_signal(barrier, inc=1, device_id=device(a, m, z), device_id_type=MESH))

    for load in loads[:3]:
        load.wait()
    pack_rows(spec_ref, station_ref, window_ref, send_ref)
    rows_ref[z, me] = send_ref[me]
    for load in loads[3:]:
        load.wait()
    pl.semaphore_wait(barrier, LAYER - 1 + 4)

    def piece_copy(along, across):
        return pltpu.make_async_remote_copy(
            src_ref=send_ref.at[along * NG + across], dst_ref=rows_ref.at[z, me],
            send_sem=piece_send, recv_sem=piece_recv.at[lax.div(x, NX // HALVES)],
            device_id=device(along, across, z), device_id_type=MESH,
        )

    def index_copy(along, across):
        return pltpu.make_async_remote_copy(
            src_ref=index_ref.at[me], dst_ref=index_ref.at[me],
            send_sem=index_send, recv_sem=index_recv,
            device_id=device(along, across, z), device_id_type=MESH,
        )

    def cross_copy(along, across):
        return pltpu.make_async_remote_copy(
            src_ref=cross_ref.at[along * NG + across], dst_ref=got_ref.at[me],
            send_sem=cross_send, recv_sem=cross_recv.at[x],
            device_id=device(along, across, z), device_id_type=MESH,
        )

    each_peer(lambda a, m: piece_copy(a, m).start())
    index_ref[me] = locate(pair_ref, tiles_ref, owner_ref, group)
    table_angles(c8_ref, s8_ref, dc_ref, ds_ref, base_ref)
    each_peer(lambda a, m: index_copy(a, m).start())

    def table_part(start, stop):
        build_table(start, stop, table_ref, c8_ref, s8_ref, dc_ref, ds_ref, base_ref)

    def ring_copy(way, distance, s, chunk, step):
        part = pl.ds(PART * s, PART)
        return pltpu.make_async_remote_copy(
            src_ref=rows_ref.at[chunk, part], dst_ref=rows_ref.at[chunk, part],
            send_sem=ring_send, recv_sem=ring_recv.at[way, distance, s],
            device_id=device(x, member, layer_at(step if way == 0 else -step)), device_id_type=MESH,
        )

    def widen(chunk, s):
        start = pl.multiple_of((chunk * LAYER + s * PART) * STA, 128)
        rows = rows_ref[chunk, pl.ds(PART * s, PART)].astype(F32)
        wide_ref[pl.ds(start, PART * STA), :] = rows.reshape(PART * STA, 128)

    def chunk_of(way, distance):
        return lax.rem(z + NZ - distance, NZ) if way == 0 else lax.rem(z + distance, NZ)

    def half(k):
        return lax.rem(lax.div(x, 2) + k, HALVES)

    def start_half(k, carry):
        s = half(k)

        @pl.when(k == 0)
        def _():
            arrived(rows_ref.at[z, pl.ds(PART * s, PART - 1)], piece_recv.at[s])

        @pl.when(k == 1)
        def _():
            arrived(rows_ref.at[z, pl.ds(PART * s, PART)], piece_recv.at[s])

        for way in range(2):
            ring_copy(way, 2, s, z, 2).start()
            ring_copy(way, 1, s, z, 1).start()
        return carry

    lax.fori_loop(0, HALVES, start_half, 0)
    for s in range(HALVES):
        widen(z, s)
    table_part(0, 6)

    arrived(index_ref.at[pl.ds(0, LAYER - 1)], index_recv)
    to_scalar = pltpu.make_async_copy(index_ref, place_ref, local_sem)
    to_scalar.start()

    def stop(i, carry):
        distance = 2 * i + 2

        def one_half(k, c):
            s = half(k)
            for way in range(2):
                chunk = chunk_of(way, distance)

                @pl.when((distance < 8) | (k == way))
                def _():
                    ring_copy(way, distance, s, chunk, 2).wait_recv()

                @pl.when((distance < 6) | ((distance == 6) & (k == way)))
                def _():
                    ring_copy(way, distance + 2, s, chunk, 2).start()

                @pl.when(distance < 8)
                def _():
                    ring_copy(way, distance + 1, s, chunk, 1).start()

                @pl.when((distance < 8) | (k == way))
                def _():
                    widen(chunk, s)
            return c

        lax.fori_loop(0, HALVES, one_half, 0)

        def odd_half(k, c):
            s = half(k)
            for way in range(2):
                chunk = chunk_of(way, distance - 1)
                ring_copy(way, distance - 1, s, chunk, 1).wait_recv()
                widen(chunk, s)
            return c

        lax.fori_loop(0, HALVES, odd_half, 0)

        @pl.when(distance < 8)
        def _():
            table_part(6 + 9 * i, jnp.minimum(15 + 9 * i, LAYER))

        return carry

    lax.fori_loop(0, 4, stop, 0)
    to_scalar.wait()

    lane = iota((2 * PPD, 128), 1)
    odd = lax.rem(lax.div(lane, 32), 2) == 1
    low = iota((PPD // 2, 128), 1) < 64
    sign = jnp.where(lane < 64, -1.0, 1.0)

    first_ref[...] = jnp.zeros((2 * PPD, 128), F32)
    second_ref[...] = jnp.zeros((2 * PPD, 128), F32)

    def correlate(j, carry):
        a, b = first_ref[...], second_ref[...]
        last, before = carry
        now = []
        for i in range(2):
            turn = jnp.minimum(2 * j, LAYER - 2) + i
            along, over = column(lax.div(turn, NG)), across(lax.rem(turn, NG))
            number = along * NG + over
            now.append((along, over))
            for k in range(PPD):
                first = place_ref[number, 0, k] & (TOTAL - 1)
                second = place_ref[number, 0, PPD + k] & (TOTAL - 1)
                first_ref[PPD * i + k : PPD * i + k + 1, :] = wide_ref[pl.ds(first, 1), :]
                second_ref[PPD * i + k : PPD * i + k + 1, :] = wide_ref[pl.ds(second, 1), :]
        real, imag = a * b, a * (pltpu.roll(b, 64, 1) * sign)
        kept, moved = jnp.where(odd, imag, real), jnp.where(odd, real, imag)
        both = kept + pltpu.roll(moved, 96, 1)
        both = both + pltpu.roll(both, 64, 1)
        for i in range(2):
            top = both[PPD * i : PPD * i + PPD // 2]
            packed = jnp.where(low, top, both[PPD * i + PPD // 2 : PPD * i + PPD])
            cross_ref[last[i][0] * NG + last[i][1]] = packed.astype(BF16).reshape(3, 8, 128)

        @pl.when(j > 1)
        def _():
            for i in range(2):
                cross_copy(*before[i]).start()

        return tuple(now), last

    begin = tuple((column(0), across(i)) for i in range(2))
    final, _ = lax.fori_loop(0, LAYER // 2 + 1, correlate, (begin, begin))
    total_ref[...] = jnp.zeros((PPD, NFFT), F32)
    got_ref[me] = cross_ref[me]
    cross_copy(*final[0]).start()

    scale = 1.0 / math.sqrt(HALF * W)
    depth = 2 * HALF // NX

    def product(t, carry):
        along = column(t)
        base = along * NG

        @pl.when(t < NX - 1)
        def _():
            arrived(got_ref.at[pl.ds(base, NG)], cross_recv.at[along])

        @pl.when(t == NX - 1)
        def _():
            arrived(got_ref.at[pl.ds(base, NG - 1)], cross_recv.at[along])

        for i in range(NG // 2):
            one = got_ref[base + 2 * i].astype(F32).reshape(PPD // 2, 128)
            two = got_ref[base + 2 * i + 1].astype(F32).reshape(PPD // 2, 128)
            top = jnp.where(low, one, pltpu.roll(two, 64, 1))
            bottom = jnp.where(low, pltpu.roll(one, 64, 1), two)
            left_ref[:, 128 * i : 128 * i + 128] = jnp.concatenate([top, bottom], axis=0).astype(BF16)
        rows = pl.ds(pl.multiple_of(base * (depth // NG), depth), depth)

        def columns(n, c):
            cols = pl.ds(pl.multiple_of(256 * n, 256), 256)
            total_ref[:, cols] += jnp.dot(left_ref[...], table_ref[rows, cols], preferred_element_type=F32)
            return c

        lax.fori_loop(0, 8, columns, 0)
        return carry

    lax.fori_loop(0, NX, product, 0)
    out_ref[...] = total_ref[:, :LAGS] * scale

    left(send_ref.at[pl.ds(0, LAYER - 1)], piece_send)
    left(index_ref.at[pl.ds(0, LAYER - 1)], index_send)
    left(cross_ref.at[pl.ds(0, LAYER - 1)], cross_send)
    left(rows_ref.at[pl.ds(0, NZ - 1)], ring_send)


def on_device(spectra, row_station, row_window, station_owner, tile_stations, pair_index):
    vmem = pl.BlockSpec(memory_space=pltpu.VMEM)
    dma = pltpu.SemaphoreType.DMA
    result = pl.pallas_call(
        kernel,
        out_shape=jax.ShapeDtypeStruct((PPD, LAGS), F32),
        in_specs=[pl.BlockSpec(memory_space=pltpu.HBM)] * 6,
        out_specs=vmem,
        scratch_shapes=[
            pltpu.VMEM((2 * STA, NFFT), BF16),
            pltpu.VMEM((1, 2 * STA), I32),
            pltpu.VMEM((1, 2 * STA), I32),
            pltpu.VMEM((32, 128), I32),
            pltpu.VMEM((NX * NZ, NG * PPD), I32),
            pltpu.VMEM((2, PPD), I32),
            pltpu.VMEM((LAYER, STA, 128), BF16),
            pltpu.VMEM((NZ, LAYER, STA, 128), BF16),
            pltpu.VMEM((TOTAL, 128), F32),
            pltpu.VMEM((LAYER, 1, 128), I32),
            pltpu.SMEM((LAYER, 1, 128), I32),
            pltpu.VMEM((2 * PPD, 128), F32),
            pltpu.VMEM((2 * PPD, 128), F32),
            pltpu.VMEM((LAYER, 3, 8, 128), BF16),
            pltpu.VMEM((LAYER, 3, 8, 128), BF16),
            pltpu.VMEM((PPD, NFFT // NX), BF16),
            pltpu.VMEM((PPD, NFFT), F32),
            pltpu.VMEM((NFFT, NFFT), BF16),
            pltpu.VMEM((128, 128), F32),
            pltpu.VMEM((128, 128), F32),
            pltpu.VMEM((16, 8, 128), F32),
            pltpu.VMEM((16, 8, 128), F32),
            pltpu.VMEM((2, 8, 128), F32),
            dma,
            dma((HALVES,)),
            dma,
            dma,
            dma,
            dma((NX,)),
            dma,
            dma((2, 9, HALVES)),
            dma((6,)),
            dma,
        ],
        compiler_params=pltpu.CompilerParams(
            collective_id=0, has_side_effects=True, vmem_limit_bytes=48 * 1024 * 1024
        ),
    )(*[pltpu.with_memory_space_constraint(v, pltpu.HBM) for v in (
        spectra.reshape(2 * STA, NFFT),
        row_station.reshape(1, 2 * STA),
        row_window.reshape(1, 2 * STA),
        station_owner.reshape(32, 128),
        tile_stations,
        pair_index.reshape(2, PPD),
    )])
    return result.reshape(1, 1, PPD, LAGS)


def solution(mesh):
    placed = (
        P(("pairs", "grp"), None, None),
        P(("pairs", "grp")),
        P(("pairs", "grp")),
        P(),
        P(),
        P("pairs", "grp", None, None),
    )
    return jax.shard_map(
        on_device,
        mesh=mesh,
        in_specs=placed,
        out_specs=P("pairs", "grp", None, None),
        check_vma=False,
    )
```

```python
import math

import jax
import jax.numpy as jnp
from jax import lax
from jax.experimental import pallas as pl
from jax.experimental.pallas import tpu as pltpu
from jax.sharding import PartitionSpec as P

MESH = pl.DeviceIdType.MESH
W = 2
NFFT = 2048
HALF = 1024
MAXLAG = 1000
LAGS = 2001
EPS = 1e-06
NX = 4
NZ = 16
NG = 8
LAYER = NX * NG
STA = 8
PPD = 48
TOTAL = NZ * LAYER * STA
HALVES = 2
PART = LAYER // HALVES
STEP = 2.0 * math.pi / NFFT
F32 = jnp.float32
I32 = jnp.int32
BF16 = jnp.bfloat16


def iota(shape, axis):
    return lax.broadcasted_iota(I32, shape, axis)


def angle(steps):
    return lax.rem(steps, NFFT).astype(F32) * STEP


def diagonal_column(row, size):
    same = iota((size, size), 0) == iota((size, size), 1)
    return jnp.sum(jnp.where(same, jnp.broadcast_to(row, (size, size)), 0), axis=1, keepdims=True)


def pack_rows(spec_ref, station_ref, window_ref, send_ref):
    station = station_ref[...]
    column = diagonal_column(station, 2 * STA)
    ahead = jnp.sum(jnp.where(column < station, 1, 0), axis=0, keepdims=True)
    place = window_ref[...] * STA + lax.div(ahead, W)
    order = jnp.where(iota((2 * STA, 2 * STA), 0) == place, 1.0, 0.0).astype(BF16)
    group = lax.div(iota((STA, 128), 1), 32)
    for tile in range(8):
        real = spec_ref[:, 128 * tile : 128 * tile + 128].astype(F32)
        imag = spec_ref[:, HALF + 128 * tile : HALF + 128 * tile + 128].astype(F32)
        power = jnp.sum(real * real + imag * imag, axis=1, keepdims=True) * (1.0 / 128)
        scale = lax.rsqrt(power + EPS)
        real = jnp.dot(order, (real * scale).astype(BF16), preferred_element_type=F32)
        imag = jnp.dot(order, (imag * scale).astype(BF16), preferred_element_type=F32)
        parts = (real[:STA], real[STA:], imag[:STA], imag[STA:])
        for quarter in range(4):
            piece = None
            for k in range(4):
                shift = (32 * (k - quarter)) % 128
                moved = pltpu.roll(parts[k], shift, 1) if shift else parts[k]
                piece = moved if piece is None else jnp.where(group == k, moved, piece)
            send_ref[4 * tile + quarter] = piece.astype(BF16)


def locate(pair_ref, tiles_ref, owner_ref, group):
    ends = 2 * PPD
    pairs = pair_ref[...]
    place = jnp.concatenate([diagonal_column(pairs[h : h + 1], PPD) for h in range(2)], axis=0)
    lanes = iota((ends, 128), 1)
    stations = tiles_ref[pl.ds(group, 1), :]
    found = jnp.zeros((ends, 128), I32)
    for c in range(3):
        found += jnp.where(place == lanes + 128 * c, stations[:, 128 * c : 128 * c + 128], 0)
    station = jnp.sum(found, axis=1, keepdims=True)
    found = jnp.zeros((ends, 128), I32)
    for c in range(32):
        found += jnp.where(station == lanes + 128 * c, owner_ref[c : c + 1, :], 0)
    owner = jnp.sum(found, axis=1, keepdims=True)
    found = jnp.zeros((ends, 128), I32)
    for c in range(32):
        ahead = (owner_ref[c : c + 1, :] == owner) & (lanes + 128 * c < station)
        found += jnp.where(ahead, 1, 0)
    rank = jnp.sum(found, axis=1, keepdims=True)
    part, member = lax.div(owner, NG), lax.rem(owner, NG)
    row = (lax.rem(part, NZ) * LAYER + lax.div(part, NZ) * NG + member) * STA + rank
    spread = jnp.where(iota((ends, 128), 0) == lanes, jnp.broadcast_to(row, (ends, 128)), 0)
    return jnp.sum(spread, axis=0, keepdims=True)


def table_angles(c8_ref, s8_ref, dc_ref, ds_ref, base_ref):
    shift = NFFT - MAXLAG
    sub, lane = iota((8, 128), 0), iota((8, 128), 1)
    fine = angle(sub * (lane + shift))
    base_ref[0] = jnp.cos(fine)
    base_ref[1] = jnp.sin(fine)
    coarse = angle(8 * iota((128, 128), 0) * (iota((128, 128), 1) + shift))
    c8_ref[...] = jnp.cos(coarse)
    s8_ref[...] = jnp.sin(coarse)
    for j in range(16):
        turn = angle(128 * j * sub)
        dc_ref[j] = jnp.cos(turn)
        ds_ref[j] = jnp.sin(turn)


def build_table(start, stop, table_ref, c8_ref, s8_ref, dc_ref, ds_ref, base_ref):
    def block(u, carry):
        c0, s0 = base_ref[0], base_ref[1]
        for h in range(2):
            base = []
            for q in range(2):
                v = 4 * u + 2 * h + q
                cv, sv = c8_ref[pl.ds(v, 1), :], s8_ref[pl.ds(v, 1), :]
                c, s = cv * c0 - sv * s0, sv * c0 + cv * s0
                base.append((c, s, -c, -s))
            for j in range(16):
                dc, ds = dc_ref[j], ds_ref[j]
                reals, imags = [], []
                for q in range(2):
                    c, s, nc, ns = base[q]
                    if q == 1 and j % 2 == 1:
                        c, s, nc, ns = nc, ns, c, s
                    reals.append(c * dc - s * ds)
                    imags.append(ns * dc + nc * ds)
                top = pl.multiple_of(64 * u + 16 * h, 16)
                low = pl.multiple_of(64 * u + 32 + 16 * h, 16)
                cols = slice(128 * j, 128 * j + 128)
                table_ref[pl.ds(top, 16), cols] = jnp.concatenate(reals, axis=0).astype(BF16)
                table_ref[pl.ds(low, 16), cols] = jnp.concatenate(imags, axis=0).astype(BF16)
        return carry

    lax.fori_loop(start, stop, block, 0)


def kernel(
    spec_hbm, station_hbm, window_hbm, owner_hbm, tiles_hbm, pair_hbm, out_ref,
    spec_ref, station_ref, window_ref, owner_ref, tiles_ref, pair_ref,
    send_ref, rows_ref, wide_ref, index_ref, place_ref, first_ref, second_ref, cross_ref, got_ref, left_ref, total_ref,
    table_ref, c8_ref, s8_ref, dc_ref, ds_ref, base_ref,
    piece_send, piece_recv, index_send, index_recv, cross_send, cross_recv, ring_send, ring_recv, load_sem, local_sem,
):
    group, member = lax.axis_index("pairs"), lax.axis_index("grp")
    x, z = lax.div(group, NZ), lax.rem(group, NZ)
    me = x * NG + member
    sources = (spec_hbm, station_hbm, window_hbm, owner_hbm, tiles_hbm, pair_hbm)
    targets = (spec_ref, station_ref, window_ref, owner_ref, tiles_ref, pair_ref)
    loads = [pltpu.make_async_copy(a, b, load_sem.at[n]) for n, (a, b) in enumerate(zip(sources, targets))]
    for load in loads:
        load.start()

    def device(along, across, layer):
        return (along * NZ + layer, across)

    def column(t):
        return lax.rem(x + jnp.where(t == 0, 2, jnp.where(t == 1, 1, jnp.where(t == 2, 3, 0))), NX)

    def across(m):
        return lax.rem(member + 2 * NG - 1 - m, NG)

    def each_peer(act):
        def one_column(t, carry):
            along = column(t)

            def one(m, c):
                act(along, across(m))
                return c

            return lax.fori_loop(0, jnp.where(t < NX - 1, NG, NG - 1), one, carry)

        lax.fori_loop(0, NX, one_column, 0)

    def layer_at(offset):
        return lax.rem(z + NZ + offset, NZ)

    def arrived(ref, sem):
        pltpu.make_async_remote_copy(
            src_ref=ref, dst_ref=ref, send_sem=piece_send, recv_sem=sem,
            device_id=device(x, member, layer_at(1)), device_id_type=MESH,
        ).wait_recv()

    def left(ref, sem):
        pltpu.make_async_remote_copy(
            src_ref=ref, dst_ref=ref, send_sem=sem, recv_sem=index_recv,
            device_id=device(x, member, layer_at(1)), device_id_type=MESH,
        ).wait_send()

    barrier = pltpu.get_barrier_semaphore()

    for offset in (2, -2, 1, -1):
        pl.semaphore_signal(barrier, inc=1, device_id=device(x, member, layer_at(offset)), device_id_type=MESH)
    each_peer(lambda a, m: pl.semaphore_signal(barrier, inc=1, device_id=device(a, m, z), device_id_type=MESH))

    for load in loads[:3]:
        load.wait()
    pack_rows(spec_ref, station_ref, window_ref, send_ref)
    rows_ref[z, me] = send_ref[me]
    for load in loads[3:]:
        load.wait()
    pl.semaphore_wait(barrier, LAYER - 1 + 4)

    def piece_copy(along, across):
        return pltpu.make_async_remote_copy(
            src_ref=send_ref.at[along * NG + across], dst_ref=rows_ref.at[z, me],
            send_sem=piece_send, recv_sem=piece_recv.at[lax.div(x, NX // HALVES)],
            device_id=device(along, across, z), device_id_type=MESH,
        )

    def index_copy(along, across):
        return pltpu.make_async_remote_copy(
            src_ref=index_ref.at[me], dst_ref=index_ref.at[me],
            send_sem=index_send, recv_sem=index_recv,
            device_id=device(along, across, z), device_id_type=MESH,
        )

    def cross_copy(along, across):
        return pltpu.make_async_remote_copy(
            src_ref=cross_ref.at[along * NG + across], dst_ref=got_ref.at[me],
            send_sem=cross_send, recv_sem=cross_recv.at[x],
            device_id=device(along, across, z), device_id_type=MESH,
        )

    each_peer(lambda a, m: piece_copy(a, m).start())
    index_ref[me] = locate(pair_ref, tiles_ref, owner_ref, group)
    each_peer(lambda a, m: index_copy(a, m).start())
    table_angles(c8_ref, s8_ref, dc_ref, ds_ref, base_ref)

    def table_part(start, stop):
        build_table(start, stop, table_ref, c8_ref, s8_ref, dc_ref, ds_ref, base_ref)

    def ring_copy(way, distance, s, chunk, step):
        part = pl.ds(PART * s, PART)
        return pltpu.make_async_remote_copy(
            src_ref=rows_ref.at[chunk, part], dst_ref=rows_ref.at[chunk, part],
            send_sem=ring_send, recv_sem=ring_recv.at[way, distance, s],
            device_id=device(x, member, layer_at(step if way == 0 else -step)), device_id_type=MESH,
        )

    def widen(chunk, s):
        start = pl.multiple_of((chunk * LAYER + s * PART) * STA, 128)
        rows = rows_ref[chunk, pl.ds(PART * s, PART)].astype(F32)
        wide_ref[pl.ds(start, PART * STA), :] = rows.reshape(PART * STA, 128)

    def chunk_of(way, distance):
        return lax.rem(z + NZ - distance, NZ) if way == 0 else lax.rem(z + distance, NZ)

    def half(k):
        return lax.rem(lax.div(x, 2) + k, HALVES)

    def start_half(k, carry):
        s = half(k)

        @pl.when(k == 0)
        def _():
            arrived(rows_ref.at[z, pl.ds(PART * s, PART - 1)], piece_recv.at[s])

        @pl.when(k == 1)
        def _():
            arrived(rows_ref.at[z, pl.ds(PART * s, PART)], piece_recv.at[s])

        for way in range(2):
            ring_copy(way, 2, s, z, 2).start()
            ring_copy(way, 1, s, z, 1).start()
        return carry

    lax.fori_loop(0, HALVES, start_half, 0)
    for s in range(HALVES):
        widen(z, s)
    table_part(0, 6)

    arrived(index_ref.at[pl.ds(0, LAYER - 1)], index_recv)
    to_scalar = pltpu.make_async_copy(index_ref, place_ref, local_sem)
    to_scalar.start()

    def stop(i, carry):
        distance = 2 * i + 2

        def one_half(k, c):
            s = half(k)
            for way in range(2):
                chunk = chunk_of(way, distance)

                @pl.when((distance < 8) | (k == way))
                def _():
                    ring_copy(way, distance, s, chunk, 2).wait_recv()

                @pl.when((distance < 6) | ((distance == 6) & (k == way)))
                def _():
                    ring_copy(way, distance + 2, s, chunk, 2).start()

                @pl.when(distance < 8)
                def _():
                    ring_copy(way, distance + 1, s, chunk, 1).start()

                @pl.when((distance < 8) | (k == way))
                def _():
                    widen(chunk, s)
            return c

        lax.fori_loop(0, HALVES, one_half, 0)

        def odd_half(k, c):
            s = half(k)
            for way in range(2):
                chunk = chunk_of(way, distance - 1)
                ring_copy(way, distance - 1, s, chunk, 1).wait_recv()
                widen(chunk, s)
            return c

        lax.fori_loop(0, HALVES, odd_half, 0)

        @pl.when(distance < 8)
        def _():
            table_part(6 + 9 * i, jnp.minimum(15 + 9 * i, LAYER))

        return carry

    lax.fori_loop(0, 4, stop, 0)
    to_scalar.wait()

    lane = iota((2 * PPD, 128), 1)
    odd = lax.rem(lax.div(lane, 32), 2) == 1
    low = iota((PPD // 2, 128), 1) < 64
    sign = jnp.where(lane < 64, -1.0, 1.0)

    first_ref[...] = jnp.zeros((2 * PPD, 128), F32)
    second_ref[...] = jnp.zeros((2 * PPD, 128), F32)

    def correlate(j, carry):
        a, b = first_ref[...], second_ref[...]
        last, before = carry
        now = []
        for i in range(2):
            turn = jnp.minimum(2 * j, LAYER - 2) + i
            along, over = column(lax.div(turn, NG)), across(lax.rem(turn, NG))
            number = along * NG + over
            now.append((along, over))
            for k in range(PPD):
                first = place_ref[number, 0, k] & (TOTAL - 1)
                second = place_ref[number, 0, PPD + k] & (TOTAL - 1)
                first_ref[PPD * i + k : PPD * i + k + 1, :] = wide_ref[pl.ds(first, 1), :]
                second_ref[PPD * i + k : PPD * i + k + 1, :] = wide_ref[pl.ds(second, 1), :]
        real, imag = a * b, a * (pltpu.roll(b, 64, 1) * sign)
        kept, moved = jnp.where(odd, imag, real), jnp.where(odd, real, imag)
        both = kept + pltpu.roll(moved, 96, 1)
        both = both + pltpu.roll(both, 64, 1)
        for i in range(2):
            top = both[PPD * i : PPD * i + PPD // 2]
            packed = jnp.where(low, top, both[PPD * i + PPD // 2 : PPD * i + PPD])
            cross_ref[last[i][0] * NG + last[i][1]] = packed.astype(BF16).reshape(3, 8, 128)

        @pl.when(j > 1)
        def _():
            for i in range(2):
                cross_copy(*before[i]).start()

        return tuple(now), last

    begin = tuple((column(0), across(i)) for i in range(2))
    final, _ = lax.fori_loop(0, LAYER // 2 + 1, correlate, (begin, begin))
    total_ref[...] = jnp.zeros((PPD, NFFT), F32)
    got_ref[me] = cross_ref[me]
    cross_copy(*final[0]).start()

    scale = 1.0 / math.sqrt(HALF * W)
    depth = 2 * HALF // NX

    def product(t, carry):
        along = column(t)
        base = along * NG

        @pl.when(t < NX - 1)
        def _():
            arrived(got_ref.at[pl.ds(base, NG)], cross_recv.at[along])

        @pl.when(t == NX - 1)
        def _():
            arrived(got_ref.at[pl.ds(base, NG - 1)], cross_recv.at[along])

        for i in range(NG // 2):
            one = got_ref[base + 2 * i].astype(F32).reshape(PPD // 2, 128)
            two = got_ref[base + 2 * i + 1].astype(F32).reshape(PPD // 2, 128)
            top = jnp.where(low, one, pltpu.roll(two, 64, 1))
            bottom = jnp.where(low, pltpu.roll(one, 64, 1), two)
            left_ref[:, 128 * i : 128 * i + 128] = jnp.concatenate([top, bottom], axis=0).astype(BF16)
        rows = pl.ds(pl.multiple_of(base * (depth // NG), depth), depth)

        def columns(n, c):
            cols = pl.ds(pl.multiple_of(256 * n, 256), 256)
            total_ref[:, cols] += jnp.dot(left_ref[...], table_ref[rows, cols], preferred_element_type=F32)
            return c

        lax.fori_loop(0, 8, columns, 0)
        return carry

    lax.fori_loop(0, NX, product, 0)
    out_ref[...] = total_ref[:, :LAGS] * scale

    left(send_ref.at[pl.ds(0, LAYER - 1)], piece_send)
    left(index_ref.at[pl.ds(0, LAYER - 1)], index_send)
    left(cross_ref.at[pl.ds(0, LAYER - 1)], cross_send)
    left(rows_ref.at[pl.ds(0, NZ - 1)], ring_send)


def on_device(spectra, row_station, row_window, station_owner, tile_stations, pair_index):
    vmem = pl.BlockSpec(memory_space=pltpu.VMEM)
    dma = pltpu.SemaphoreType.DMA
    result = pl.pallas_call(
        kernel,
        out_shape=jax.ShapeDtypeStruct((PPD, LAGS), F32),
        in_specs=[pl.BlockSpec(memory_space=pltpu.HBM)] * 6,
        out_specs=vmem,
        scratch_shapes=[
            pltpu.VMEM((2 * STA, NFFT), BF16),
            pltpu.VMEM((1, 2 * STA), I32),
            pltpu.VMEM((1, 2 * STA), I32),
            pltpu.VMEM((32, 128), I32),
            pltpu.VMEM((NX * NZ, NG * PPD), I32),
            pltpu.VMEM((2, PPD), I32),
            pltpu.VMEM((LAYER, STA, 128), BF16),
            pltpu.VMEM((NZ, LAYER, STA, 128), BF16),
            pltpu.VMEM((TOTAL, 128), F32),
            pltpu.VMEM((LAYER, 1, 128), I32),
            pltpu.SMEM((LAYER, 1, 128), I32),
            pltpu.VMEM((2 * PPD, 128), F32),
            pltpu.VMEM((2 * PPD, 128), F32),
            pltpu.VMEM((LAYER, 3, 8, 128), BF16),
            pltpu.VMEM((LAYER, 3, 8, 128), BF16),
            pltpu.VMEM((PPD, NFFT // NX), BF16),
            pltpu.VMEM((PPD, NFFT), F32),
            pltpu.VMEM((NFFT, NFFT), BF16),
            pltpu.VMEM((128, 128), F32),
            pltpu.VMEM((128, 128), F32),
            pltpu.VMEM((16, 8, 128), F32),
            pltpu.VMEM((16, 8, 128), F32),
            pltpu.VMEM((2, 8, 128), F32),
            dma,
            dma((HALVES,)),
            dma,
            dma,
            dma,
            dma((NX,)),
            dma,
            dma((2, 9, HALVES)),
            dma((6,)),
            dma,
        ],
        compiler_params=pltpu.CompilerParams(
            collective_id=0, has_side_effects=True, vmem_limit_bytes=48 * 1024 * 1024
        ),
    )(*[pltpu.with_memory_space_constraint(v, pltpu.HBM) for v in (
        spectra.reshape(2 * STA, NFFT),
        row_station.reshape(1, 2 * STA),
        row_window.reshape(1, 2 * STA),
        station_owner.reshape(32, 128),
        tile_stations,
        pair_index.reshape(2, PPD),
    )])
    return result.reshape(1, 1, PPD, LAGS)


def solution(mesh):
    placed = (
        P(("pairs", "grp"), None, None),
        P(("pairs", "grp")),
        P(("pairs", "grp")),
        P(),
        P(),
        P("pairs", "grp", None, None),
    )
    return jax.shard_map(
        on_device,
        mesh=mesh,
        in_specs=placed,
        out_specs=P("pairs", "grp", None, None),
        check_vma=False,
    )
```
